256 devices in a mesh: sec: 2 (over core), clu: 8 (over x, y_hi), blk: 16 (over y_lo, z).
Axes of the slice: x: 4, y: 4 (y_hi: 2, y_lo: 2; y = y_hi * 2 + y_lo), z: 8, core: 2. Of those that a mesh axis runs over, the one named last changes fastest.
Arguments:
- right_side: float32 [32, 128, 128, 128], P(None, ('sec', 'clu'), 'blk'), may hold values from -18 to 18
- block_weight: float32 [128, 128], P(('sec', 'clu'), 'blk'), may hold values from 2 to 8
- across_weight: float32 [128, 128], P(('sec', 'clu'), 'blk'), may hold values from 0.3 to 1
- along_weight: float32 [128, 128], P(('sec', 'clu'), 'blk'), may hold values from 0.3 to 1
- block_stiffness: bfloat16 [128, 128], replicated, may hold values from -0.1 to 1.1, as said below
- across_matrix: bfloat16 [128, 128], replicated, may hold values from -0.044194174 to 0.044194174
- along_matrix: bfloat16 [128, 128], replicated, may hold values from -0.044194174 to 0.044194174
- boundary_blocks: bfloat16 [2, 8, 768, 128, 128], P('sec', 'clu', 'blk'), may hold values from -0.22949219 to 0.22949219
- block_rows: int32 [2, 8, 768], P('sec', 'clu', 'blk'), may hold values from 0 to 31
- block_columns: int32 [2, 8, 768], P('sec', 'clu', 'blk'), may hold values from 0 to 15
- live_pairs: int32 [2, 8, 16], P('sec', 'clu', 'blk'), may hold values from 12 to 48, as said below
- surface_index: int32 [2, 8, 2048], P('sec', 'clu', 'blk'), may hold values from 0 to 8191, as said below
- interface_slot: int32 [32768], P('clu'), may hold values from 0 to 4095, as said below
Outputs:
- solution: float32 [32, 128, 128, 128], P(None, ('sec', 'clu'), 'blk')
The draws below stay inside these ranges and needn't reach their ends.
Inputs may be any that keep to these rules, and one draw needn't show every extreme that they name: `block_stiffness`: symmetric. The first live_pairs[s, c, j] of a device's 48 listed pairs are live; some device has all 48 live. `surface_index`: the 128 entries of one device are distinct local dof numbers of that device. `interface_slot`: within each row range of 4096 interface dofs, each slot is taken exactly once.
All inputs are finite; a program needn't handle non-finite values.
Results may differ from the reference program's by a relative error of at most 0.0003.
The reference program's roundings to bfloat16 on the way count: a program that leaves them out, or rounds other values in their place, can miss the bound.
Values may be sent and summed in bfloat16 or wider, within the bound.
No kernel may reach another device: no remote copies, remote signals or barrier semaphores. Data moves between devices by JAX's collectives and lax.ppermute only.
A program may use at most 64 MiB of HBM per device.

```python
import math
import jax
import jax.numpy as jnp
from jax import lax

P_SIZE = 128
CL = 128
CASES = 32
BX = 8
BY = 8
SURF = 128
NP = 48
ITERS = 3
NBX = 128
NBY = 128
RROWS = 4096
RCL = 32
CCL = 16
N_SEC = 2
N_CLU = 8
N_BLK = 16


def draw_block_stiffness(key, part):
    noise = jax.random.truncated_normal(key, -4.0, 4.0, (P_SIZE, P_SIZE), jnp.float32) * (0.2 / math.sqrt(2.0 * P_SIZE))
    return (jnp.eye(P_SIZE, dtype=jnp.float32) + noise + noise.T).astype(jnp.bfloat16)


def draw_across_matrix(key, part):
    return (jax.random.truncated_normal(jax.random.fold_in(key, 11), -4.0, 4.0, (P_SIZE, P_SIZE), jnp.float32) * (0.125 / math.sqrt(P_SIZE))).astype(jnp.bfloat16)


def draw_along_matrix(key, part):
    return (jax.random.truncated_normal(jax.random.fold_in(key, 23), -4.0, 4.0, (P_SIZE, P_SIZE), jnp.float32) * (0.125 / math.sqrt(P_SIZE))).astype(jnp.bfloat16)


def draw_live_pairs(key, part):
    device_count = N_SEC * N_CLU * N_BLK
    lowest = max(1, NP // 4)
    counts = jax.random.randint(jax.random.fold_in(key, 1), (device_count,), lowest, NP + 1)
    busiest = jax.random.randint(jax.random.fold_in(key, 2), (), 0, device_count)
    counts = counts.at[busiest].set(NP)
    counts = counts.at[(busiest + 1) % device_count].set(lowest)
    return counts.reshape(N_SEC, N_CLU, N_BLK).astype(jnp.int32)


def draw_surface_index(key, part):
    dof_total = BX * BY * P_SIZE
    device_count = N_SEC * N_CLU * N_BLK
    split_keys = jax.random.split(jax.random.fold_in(key, 3), device_count)
    chosen = jax.vmap(lambda subkey: jax.random.permutation(subkey, dof_total)[:SURF])(split_keys).astype(jnp.int32)
    leading = chosen[0]
    present = jnp.any(leading == dof_total - 1)
    leading = jnp.where(present, leading, leading.at[0].set(dof_total - 1))
    chosen = chosen.at[0].set(leading)
    return chosen.reshape(N_SEC, N_CLU, N_BLK * SURF)


def draw_interface_slot(key, part):
    split_keys = jax.random.split(jax.random.fold_in(key, 5), N_CLU)
    orders = jax.vmap(lambda subkey: jax.random.permutation(subkey, RROWS))(split_keys)
    return orders.reshape(N_CLU * RROWS).astype(jnp.int32)


def touch_ends(array, key, low, top_value):
    dims = array.shape
    place = [jax.random.randint(jax.random.fold_in(key, axis), (), 0, dims[axis]) for axis in range(len(dims))]
    array = array.at[tuple(place)].set(low)
    longest = dims.index(max(dims))
    place[longest] = (place[longest] + 1) % dims[longest]
    return array.at[tuple(place)].set(top_value)


def steps_of(own_key, dims, cuts, low, top_value):
    gain = 1.0
    for position, parts in cuts:
        draws = jax.random.uniform(jax.random.fold_in(jax.random.fold_in(own_key, 6), position), (parts,), jnp.float32, low / len(cuts), top_value / len(cuts))
        gain = gain * jnp.repeat(jnp.exp(draws), dims[position] // parts).reshape((-1,) + (1,) * (len(dims) - 1 - position))
    return gain


def bell_draw(stream_key, shape, deviation, bound, shards=(), kind=jnp.bfloat16):
    values = deviation * jax.random.normal(stream_key, shape, jnp.float32)
    if shards:
        values = values * steps_of(stream_key, shape, shards, -0.22, 0.18)
    return jnp.clip(values, -bound, bound).astype(kind)


def setup_inputs(seed: int = 0) -> dict:
    keys = jax.random.split(jax.random.key(seed), 14)
    right_side = bell_draw(keys[0], (CASES, NBX, NBY, P_SIZE), 3.0, 18.0, ((1, 16), (2, 16)), jnp.float32)
    block_weight = jnp.clip(jnp.exp(math.log(8.0) - 1.3862944 * jax.random.uniform(keys[1], (NBX, NBY), jnp.float32) ** steps_of(keys[1], (NBX, NBY), ((0, 16), (1, 16)), -0.2, 0.2)), 2.0, 8.0)
    across_weight = jnp.clip(jnp.exp(math.log(1.0) - 1.2039728 * jax.random.uniform(keys[2], (NBX, NBY), jnp.float32) ** steps_of(keys[2], (NBX, NBY), ((0, 16), (1, 16)), -0.2, 0.2)), 0.3, 1.0)
    along_weight = jnp.clip(jnp.exp(math.log(1.0) - 1.2039728 * jax.random.uniform(keys[3], (NBX, NBY), jnp.float32) ** steps_of(keys[3], (NBX, NBY), ((0, 16), (1, 16)), -0.2, 0.2)), 0.3, 1.0)
    block_stiffness = draw_block_stiffness(jax.random.fold_in(keys[13], 71), 0)
    across_matrix = draw_across_matrix(jax.random.fold_in(keys[13], 71), 0)
    along_matrix = draw_along_matrix(jax.random.fold_in(keys[13], 71), 0)
    boundary_blocks = bell_draw(keys[7], (N_SEC, N_CLU, N_BLK * NP, CL, CL), (3 * (CL * CL * NP / SURF) ** -0.5), 0.22949219, ((0, 2), (1, 8), (2, 16)))
    block_rows = touch_ends(jax.random.randint(keys[8], (N_SEC, N_CLU, N_BLK * NP), 0, RCL), jax.random.fold_in(keys[8], 1), 0, RCL - 1).astype(jnp.int32)
    block_columns = touch_ends(jax.random.randint(keys[9], (N_SEC, N_CLU, N_BLK * NP), 0, CCL), jax.random.fold_in(keys[9], 1), 0, CCL - 1).astype(jnp.int32)
    live_pairs = draw_live_pairs(jax.random.fold_in(keys[13], 71), 0)
    surface_index = draw_surface_index(jax.random.fold_in(keys[13], 71), 0)
    interface_slot = draw_interface_slot(jax.random.fold_in(keys[13], 71), 0)
    return dict(right_side=right_side, block_weight=block_weight, across_weight=across_weight, along_weight=along_weight, block_stiffness=block_stiffness, across_matrix=across_matrix, along_matrix=along_matrix, boundary_blocks=boundary_blocks, block_rows=block_rows, block_columns=block_columns, live_pairs=live_pairs, surface_index=surface_index, interface_slot=interface_slot)


def product(left, right):
    return jnp.einsum('cabk,kl->cabl', left.astype(jnp.float32), right.astype(jnp.float32))


def stiffness_piece(rounded, block_weight, across_weight, along_weight, block_stiffness, across_matrix, along_matrix):
    padded = jnp.pad(rounded, ((0, 0), (1, 1), (1, 1), (0, 0)))
    across_padded = jnp.pad(across_weight, ((1, 1), (1, 1)))
    along_padded = jnp.pad(along_weight, ((1, 1), (1, 1)))
    result = block_weight[None, :, :, None] * product(rounded, block_stiffness)
    result = result - across_weight[None, :, :, None] * product(padded[:, 2:, 1:-1], across_matrix)
    result = result - across_padded[None, :-2, 1:-1, None] * product(padded[:, :-2, 1:-1], across_matrix.T)
    result = result - along_weight[None, :, :, None] * product(padded[:, 1:-1, 2:], along_matrix)
    result = result - along_padded[None, 1:-1, :-2, None] * product(padded[:, 1:-1, :-2], along_matrix.T)
    return result


def stiffness_apply(rounded, block_weight, across_weight, along_weight, block_stiffness, across_matrix, along_matrix):
    group = math.gcd(CASES, 8)
    pieces = rounded.reshape(CASES // group, group, NBX, NBY, P_SIZE)

    def single(piece):
        return stiffness_piece(piece, block_weight, across_weight, along_weight, block_stiffness, across_matrix, along_matrix)

    return lax.map(single, pieces).reshape(CASES, NBX, NBY, P_SIZE)


def to_devices(field):
    shaped = field.reshape(CASES, N_SEC * N_CLU, BX, N_BLK, BY, P_SIZE)
    return shaped.transpose(1, 3, 0, 2, 4, 5).reshape(N_SEC * N_CLU, N_BLK, CASES, BX * BY * P_SIZE)


def from_devices(stacked):
    shaped = stacked.reshape(N_SEC * N_CLU, N_BLK, CASES, BX, BY, P_SIZE)
    return shaped.transpose(2, 0, 3, 1, 4, 5).reshape(CASES, NBX, NBY, P_SIZE)


def boundary_apply(rounded, boundary_blocks, block_rows, block_columns, live_pairs, surface_index, interface_slot):
    stacked = to_devices(rounded)
    surface = surface_index.reshape(N_SEC * N_CLU, N_BLK, SURF)
    traces = jax.vmap(jax.vmap(lambda field, picks: jnp.take(field, picks, axis=1)))(stacked, surface)
    traces = traces.reshape(N_SEC, N_CLU, N_BLK, CASES, SURF).transpose(1, 3, 0, 2, 4).reshape(N_CLU, CASES, RROWS)
    slots = interface_slot.reshape(N_CLU, RROWS)
    interface = jax.vmap(lambda trace, picks: jnp.take(trace, picks, axis=1))(traces, slots)
    row_tiles = interface.reshape(N_CLU, CASES, RCL, CL)
    device_count = N_SEC * N_CLU * N_BLK
    blocks = boundary_blocks.reshape(device_count, NP, CL, CL)
    rows_list = block_rows.reshape(device_count, NP)
    columns_list = block_columns.reshape(device_count, NP)
    live_list = live_pairs.reshape(device_count)
    indices = jnp.arange(device_count, dtype=jnp.int32)
    clu_of = (indices // N_BLK) % N_CLU
    blk_of = indices % N_BLK
    pair_index = jnp.arange(NP, dtype=jnp.int32)

    def column_step(total, item):
        block, rows, columns, live, clu, blk = item
        picked = jnp.take(row_tiles[clu], rows, axis=1)
        terms = jnp.einsum('cpk,pkl->cpl', picked.astype(jnp.float32), block.astype(jnp.float32))
        terms = terms * (pair_index < live).astype(jnp.float32)[None, :, None]
        return total.at[:, blk * CCL + columns].add(terms), None

    start_columns = jnp.zeros((CASES, N_BLK * CCL, CL), jnp.float32)
    column_total, _ = lax.scan(column_step, start_columns, (blocks, rows_list, columns_list, live_list, clu_of, blk_of))
    column_low = column_total.astype(jnp.bfloat16)

    def row_step(total, item):
        block, rows, columns, live, clu, blk = item
        picked = jnp.take(column_low, blk * CCL + columns, axis=1)
        terms = jnp.einsum('cpl,pkl->cpk', picked.astype(jnp.float32), block.astype(jnp.float32))
        terms = terms * (pair_index < live).astype(jnp.float32)[None, :, None]
        return total.at[:, clu * RCL + rows].add(terms), None

    start_rows = jnp.zeros((CASES, N_CLU * RCL, CL), jnp.float32)
    row_total, _ = lax.scan(row_step, start_rows, (blocks, rows_list, columns_list, live_list, clu_of, blk_of))
    ranges = row_total.reshape(CASES, N_CLU, RROWS).transpose(1, 0, 2)
    inverse = jax.vmap(lambda picks: jnp.zeros((RROWS,), jnp.int32).at[picks].set(jnp.arange(RROWS, dtype=jnp.int32)))(slots)
    slot_values = jax.vmap(lambda values, picks: jnp.take(values, picks, axis=1))(ranges, inverse)
    slot_values = slot_values.reshape(N_CLU, CASES, N_SEC, N_BLK, SURF).transpose(2, 0, 3, 1, 4)
    slot_values = slot_values.reshape(N_SEC * N_CLU, N_BLK, CASES, SURF)
    empty = jnp.zeros((N_SEC * N_CLU, N_BLK, CASES, BX * BY * P_SIZE), jnp.float32)
    filled = jax.vmap(jax.vmap(lambda field, picks, values: field.at[:, picks].add(values)))(empty, surface, slot_values)
    return from_devices(filled)


def reference(right_side, block_weight, across_weight, along_weight, block_stiffness, across_matrix, along_matrix, boundary_blocks, block_rows, block_columns, live_pairs, surface_index, interface_slot):
    solution = jnp.zeros_like(right_side)
    residual = right_side
    direction = right_side
    norm_now = jnp.sum(residual * residual, axis=(1, 2, 3))
    for iteration in range(ITERS):
        rounded = direction.astype(jnp.bfloat16)
        image_field = stiffness_apply(rounded, block_weight, across_weight, along_weight, block_stiffness, across_matrix, along_matrix)
        image_field = image_field + boundary_apply(rounded, boundary_blocks, block_rows, block_columns, live_pairs, surface_index, interface_slot)
        curvature = jnp.sum(direction * image_field, axis=(1, 2, 3))
        alpha = (norm_now / curvature)[:, None, None, None]
        solution = solution + alpha * direction
        residual = residual - alpha * image_field
        norm_next = jnp.sum(residual * residual, axis=(1, 2, 3))
        direction = residual + (norm_next / norm_now)[:, None, None, None] * direction
        norm_now = norm_next
    return solution
```

```python
import functools

import jax
import jax.numpy as jnp
from jax import lax
from jax.experimental import pallas as pl
from jax.experimental.pallas import tpu as pltpu
from jax.sharding import Mesh
from jax.sharding import PartitionSpec as P

ITERS = 3
ALL = ("sec", "clu_0", "clu_1", "blk_0", "blk_1")
SEC_CLU = ("sec", "clu_0", "clu_1")
BLK = ("blk_0", "blk_1")
CLU = ("clu_0", "clu_1")
F32 = jnp.float32
BF16 = jnp.bfloat16
SMEM = pl.BlockSpec(memory_space=pltpu.SMEM)
VMEM = pl.BlockSpec(memory_space=pltpu.VMEM)


def passed_along(value, axis, by):
    count = lax.axis_size(axis)
    pairs = [(i, i + by) for i in range(count) if 0 <= i + by < count]
    return lax.ppermute(value, axis, pairs)


def partner(value):
    return lax.ppermute(value, "sec", [(0, 1), (1, 0)])


def exchanged(pieces, axes):
    return lax.all_to_all(pieces, axes, split_axis=0, concat_axis=0, tiled=True)


def lanes_taken(rows, index):
    return jnp.take_along_axis(rows, index, axis=1)


def like(shape, dtype=F32):
    return jax.ShapeDtypeStruct(shape, dtype)


def lane_iota(shape):
    return lax.broadcasted_iota(jnp.int32, shape, len(shape) - 1)


def row_iota(shape):
    return lax.broadcasted_iota(jnp.int32, shape, len(shape) - 2)


def column_to_row(column, at):
    cases = column.shape[0]
    shape = (cases, 128)
    here = lane_iota(shape) == row_iota(shape) + at
    return jnp.sum(jnp.where(here, column, 0.0), axis=0, keepdims=True)


def row_to_column(row, at, cases):
    shape = (cases, 128)
    here = lane_iota(shape) == row_iota(shape) + at
    return jnp.sum(jnp.where(here, row, 0.0), axis=1, keepdims=True)


def trace_of(ref, case, lane_index, block_index):
    slabs, width = ref.shape[1], ref.shape[2]
    sub = row_iota((width, 128))
    total = jnp.zeros((width, 128), F32)
    for a in range(slabs):
        picked = lanes_taken(ref[case, a], lane_index)
        total = jnp.where(block_index == a * width + sub, picked, total)
    return jnp.sum(total, axis=0, keepdims=True)


def first_trace_kernel(field_ref, surface_ref, out_ref):
    copies = out_ref.shape[0]
    lane_index = jnp.broadcast_to(surface_ref[0:1, :], (8, 128))
    block_index = jnp.broadcast_to(surface_ref[1:2, :], (8, 128))

    def step(case, carry):
        row = trace_of(field_ref, case, lane_index, block_index)
        out_ref[0, pl.ds(case, 1), :] = row
        return carry

    lax.fori_loop(0, field_ref.shape[0], step, 0, unroll=4)
    value = out_ref[0]
    for i in range(1, copies):
        out_ref[i] = value


def permuted_block(source_ref, lanes_ref, blocks_ref, d):
    count, cases = source_ref.shape[0], source_ref.shape[1]
    lane_index = jnp.broadcast_to(lanes_ref[pl.ds(d, 1), :], (8, 128))
    block_index = jnp.broadcast_to(blocks_ref[pl.ds(d, 1), :], (8, 128))
    groups = cases // 8
    totals = [jnp.zeros((8, 128), F32) for _ in range(groups)]
    for b in range(count):
        here = block_index == b
        for g in range(groups):
            picked = lanes_taken(source_ref[b, 8 * g : 8 * g + 8, :], lane_index)
            totals[g] = jnp.where(here, picked, totals[g])
    return totals


def scalars_of(pieces_ref):
    return jnp.sum(pieces_ref[...], axis=0)


def alpha_beta(sums):
    norm = sums[:, 0:1]
    curvature = sums[:, 1:2]
    alpha = norm / curvature
    following = norm - 2.0 * alpha * sums[:, 2:3] + alpha * alpha * sums[:, 3:4]
    beta = jnp.maximum(following, 0.0) / norm
    return alpha, beta


def forward_kernel(first, last, *refs):
    refs = list(refs)
    rows_ref, columns_ref, live_ref, half_ref = refs[:4]
    lanes_ref, blocks_ref, boundary_ref = refs[4:7]
    refs = refs[7:]
    if first:
        mine_ref, other_ref, direction_ref, keep_ref, send_ref, low_ref = refs[:6]
        rest = refs[6:]
        count = mine_ref.shape[0]
        direction_ref[:count] = mine_ref[...]
        direction_ref[count:] = other_ref[...]
    else:
        old_residual_ref, old_direction_ref, mine_ref, other_ref, sums_ref = refs[:5]
        if last:
            keep_ref, send_ref, direction_ref, low_ref = refs[5:9]
            rest = refs[9:]
        else:
            residual_ref, direction_ref, keep_ref, send_ref, low_ref = refs[5:10]
            rest = refs[10:]
        cases = old_direction_ref.shape[1]
        count = mine_ref.shape[0]
        alpha, beta = alpha_beta(scalars_of(sums_ref))
        alpha = jnp.broadcast_to(alpha, (cases, 128))
        beta = jnp.broadcast_to(beta, (cases, 128))
        for half, image_ref in ((0, mine_ref), (1, other_ref)):
            for i in range(count):
                b = half * count + i
                residual = old_residual_ref[b] - alpha * image_ref[i, :cases, :]
                if not last:
                    residual_ref[b] = residual
                direction_ref[b] = residual + beta * old_direction_ref[b]
    cases = direction_ref.shape[1]
    groups = cases // 8

    def step(d, carry):
        totals = permuted_block(direction_ref, lanes_ref, blocks_ref, d)
        value = jnp.concatenate(totals, axis=0)
        low = value.astype(BF16)
        if last:
            left = value - low.astype(F32)
            second = left.astype(BF16)
            low_ref[d] = jnp.concatenate([low, second], axis=0)
        else:
            low_ref[d] = low
        return carry

    lax.fori_loop(0, direction_ref.shape[0], step, 0)
    half_count = keep_ref.shape[0]
    keep_ref[...] = jnp.zeros(keep_ref.shape, F32)
    send_ref[...] = jnp.zeros(send_ref.shape, F32)
    sums_scratch = rest[0]
    sums_scratch[...] = jnp.zeros(sums_scratch.shape, F32)
    live = live_ref[0]
    flip = half_ref[0] * half_count
    for p in range(boundary_ref.shape[0]):
        product = jnp.dot(low_ref[rows_ref[p]], boundary_ref[p], preferred_element_type=F32)
        product = jnp.where(p < live, product, 0.0)
        where = columns_ref[p] ^ flip
        sums_scratch[where] += product
    keep_ref[...] = sums_scratch[:half_count]
    send_ref[...] = sums_scratch[half_count:]


def backward_kernel(
    rows_ref,
    columns_ref,
    live_ref,
    half_ref,
    lanes_ref,
    blocks_ref,
    boundary_ref,
    mine_ref,
    other_ref,
    keep_ref,
    send_ref,
    low_ref,
    rows_scratch,
):
    half_count = mine_ref.shape[0]
    low_ref[:half_count] = mine_ref[...]
    low_ref[half_count:] = other_ref[...]
    rows_scratch[...] = jnp.zeros(rows_scratch.shape, F32)
    live = live_ref[0]
    flip = half_ref[0] * half_count
    for p in range(boundary_ref.shape[0]):
        product = lax.dot_general(
            low_ref[columns_ref[p] ^ flip],
            boundary_ref[p],
            (((1,), (1,)), ((), ())),
            preferred_element_type=F32,
        )
        product = jnp.where(p < live, product, 0.0)
        rows_scratch[rows_ref[p]] += product
    count = keep_ref.shape[0]
    for at, out_ref in ((0, keep_ref), (count, send_ref)):

        def step(d, carry, at=at, out_ref=out_ref):
            totals = permuted_block(rows_scratch, lanes_ref, blocks_ref, at + d)
            for g, total in enumerate(totals):
                out_ref[d, 8 * g : 8 * g + 8, :] = total
            return carry

        lax.fori_loop(0, count, step, 0)


def stiffness_kernel(
    want_trace,
    direction_ref,
    residual_ref,
    before_ref,
    after_ref,
    left_ref,
    right_ref,
    weights_ref,
    matrices_ref,
    surface_ref,
    *out_refs,
):
    if want_trace:
        image_ref, trace_ref, dots_ref, low_ref, high_ref, sums_ref = out_refs
    else:
        dots_ref, image_ref, low_ref, high_ref, sums_ref = out_refs
    cases, slabs, width = direction_ref.shape[:3]
    rows = cases * width

    def product(value, which):
        return jnp.dot(
            value.reshape(rows, 128), matrices_ref[which], preferred_element_type=F32
        ).reshape(cases, width, 128)

    def low(a):
        if a < 0:
            return before_ref[...]
        if a == slabs:
            return after_ref[...]
        return direction_ref[:, a].astype(BF16)

    high_ref[...] = product(right_ref[...], 3)
    low_ref[...] = product(left_ref[...], 4)
    for a in range(slabs):
        own = low(a)
        result = weights_ref[0, a][None] * product(own, 0)
        result = result - weights_ref[1, a][None] * product(low(a + 1), 1)
        result = result - weights_ref[2, a][None] * product(low(a - 1), 2)
        result = result - weights_ref[3, a][None] * pltpu.roll(product(own, 3), width - 1, 1)
        result = result - weights_ref[4, a][None] * pltpu.roll(product(own, 4), 1, 1)
        result = result - weights_ref[5, a][None] * high_ref[:, a : a + 1, :]
        result = result - weights_ref[6, a][None] * low_ref[:, a : a + 1, :]
        image_ref[:, a] = result
    lane_index = jnp.broadcast_to(surface_ref[0:1, :], (8, 128))
    block_index = jnp.broadcast_to(surface_ref[1:2, :], (8, 128))

    def step(case, carry):
        r = residual_ref[case]
        d = direction_ref[case]
        q = image_ref[case]
        pairs = ((r, r), (d, q), (r, q), (q, q)) if want_trace else ((r, r), (d, q))
        for i, (one, two) in enumerate(pairs):
            sums_ref[i, pl.ds(case, 1), :] = jnp.sum(
                jnp.sum(one * two, axis=0), axis=0, keepdims=True
            )
        if want_trace:
            trace_ref[pl.ds(case, 1), :] = trace_of(image_ref, case, lane_index, block_index)
        return carry

    lax.fori_loop(0, cases, step, 0, unroll=4)
    lane = lane_iota((cases, 128))
    dots = jnp.zeros((cases, 128), F32)
    for i in range(4 if want_trace else 2):
        dots = jnp.where(lane == i, jnp.sum(sums_ref[i], axis=1, keepdims=True), dots)
    dots_ref[...] = dots


def own_kernel(
    place_ref, arrived_ref, trace_ref, dots_ref, residual_ref, direction_ref, out_ref, own_ref
):
    copies, cases = out_ref.shape[0], trace_ref.shape[0]
    y = jnp.sum(arrived_ref[...], axis=0)
    own_ref[...] = y
    trace = trace_ref[...]
    r = residual_ref[place_ref[0]]
    d = direction_ref[place_ref[0]]
    dots = dots_ref[...]
    terms = (None, d * y, r * y, (2.0 * trace + y) * y)
    row = jnp.zeros((1, 128), F32)
    for i, term in enumerate(terms):
        column = dots[:, i : i + 1]
        if term is not None:
            column = column + jnp.sum(term, axis=1, keepdims=True)
        row = row + column_to_row(column, i * cases)
    image = trace + y
    row8 = jnp.broadcast_to(row, (8, 128))
    for i in range(copies):
        out_ref[i, :cases, :] = image
        out_ref[i, cases:, :] = row8


def range_sum_kernel(mine_ref, other_ref, out_ref):
    copies, cases = out_ref.shape[0], out_ref.shape[1]
    row = jnp.sum(mine_ref[:, cases : cases + 8, :], axis=0) + jnp.sum(
        other_ref[:, cases : cases + 8, :], axis=0
    )
    row = row[0:1, :]
    lane = lane_iota((cases, 128))
    sums = jnp.zeros((cases, 128), F32)
    for i in range(4):
        sums = jnp.where(lane == i, row_to_column(row, i * cases, cases), sums)
    for i in range(copies):
        out_ref[i] = sums


def update_kernel(first, *refs):
    if first:
        sums_ref, own_ref, inverse_ref, image_ref, residual_ref, direction_ref = refs[:6]
        solution_ref = None
        refs = refs[6:]
    else:
        sums_ref, own_ref, inverse_ref, image_ref, residual_ref, direction_ref, solution_ref = refs[
            :7
        ]
        refs = refs[7:]
    new_solution_ref, new_residual_ref, new_direction_ref, alpha_ref, beta_ref = refs
    cases, slabs, width = direction_ref.shape[:3]
    alpha, beta = alpha_beta(scalars_of(sums_ref))
    alpha_ref[...] = jnp.broadcast_to(alpha, (cases, 128))
    beta_ref[...] = jnp.broadcast_to(beta, (cases, 128))

    def step(case, carry):
        alpha = jnp.broadcast_to(alpha_ref[pl.ds(case, 1), :], (width, 128))
        beta = jnp.broadcast_to(beta_ref[pl.ds(case, 1), :], (width, 128))
        own = jnp.broadcast_to(own_ref[pl.ds(case, 1), :], (width, 128))
        for a in range(slabs):
            slot = inverse_ref[a]
            there = slot > 0
            extra = lanes_taken(own, jnp.where(there, slot - 1, 0))
            image = image_ref[case, a] + jnp.where(there, extra, 0.0)
            d = direction_ref[case, a]
            r = residual_ref[case, a] - alpha * image
            new_residual_ref[case, a] = r
            moved = alpha * d
            if solution_ref is not None:
                moved = solution_ref[case, a] + moved
            new_solution_ref[case, a] = moved
            new_direction_ref[case, a] = r + beta * d
        return carry

    lax.fori_loop(0, cases, step, 0, unroll=2)


def last_sums_kernel(arrived_ref, dots_ref, out_ref):
    copies = out_ref.shape[0]
    cases = dots_ref.shape[0]
    total = jnp.sum(arrived_ref[...], axis=0)
    z = total[:cases]
    rest = total[cases:]
    low = z.astype(BF16).astype(F32)
    dots = dots_ref[...]
    curvature = dots[:, 1:2] + jnp.sum((z + rest) * low, axis=1, keepdims=True)
    row = column_to_row(dots[:, 0:1], 0) + column_to_row(curvature, cases)
    out_ref[...] = jnp.broadcast_to(row[None], (copies, 1, 128))


def final_kernel(sums_ref, direction_ref, solution_ref, out_ref, alpha_ref):
    cases, slabs, width = direction_ref.shape[:3]
    row = jnp.sum(sums_ref[...], axis=0)
    norm = row_to_column(row, 0, cases)
    curvature = row_to_column(row, cases, cases)
    alpha_ref[...] = jnp.broadcast_to(norm / curvature, (cases, 128))

    def step(case, carry):
        alpha = jnp.broadcast_to(alpha_ref[pl.ds(case, 1), :], (width, 128))
        for a in range(slabs):
            out_ref[case, a] = solution_ref[case, a] + alpha * direction_ref[case, a]
        return carry

    lax.fori_loop(0, cases, step, 0, unroll=2)


def shards(
    right_side,
    block_weight,
    across_weight,
    along_weight,
    block_stiffness,
    across_matrix,
    along_matrix,
    boundary_blocks,
    block_rows,
    block_columns,
    live_pairs,
    surface_index,
    interface_slot,
):
    cases, slabs, width, lanes = right_side.shape
    field = right_side.shape
    rows_local = block_rows[0, 0]
    columns_local = block_columns[0, 0]
    blocks_local = boundary_blocks[0, 0]
    live_local = live_pairs[0, 0]
    surface_local = surface_index[0, 0]
    half = lax.axis_index("sec").astype(jnp.int32)
    place = lax.axis_index(BLK).astype(jnp.int32)
    half_local = half.reshape(1)
    place_local = place.reshape(1)
    blk_count = lax.axis_size(BLK)
    clu_count = lax.axis_size(CLU)
    owners = 2 * blk_count
    all_count = owners * clu_count
    slot_count = interface_slot.shape[0]
    surface = jnp.stack([surface_local % lanes, surface_local // lanes])

    trace = pl.pallas_call(
        first_trace_kernel,
        out_shape=like((blk_count, cases, lanes)),
        name="first_trace",
    )(right_side, surface)
    mine = exchanged(trace, BLK)
    other = partner(mine)

    owner = (interface_slot // lanes) ^ (half * blk_count)
    slot_blocks = owner.reshape(slot_count // lanes, lanes)
    slot_lanes = (interface_slot % lanes).reshape(slot_count // lanes, lanes)
    number = jnp.arange(slot_count, dtype=jnp.int32)
    lane_number = jnp.arange(lanes, dtype=jnp.int32)
    by_owner = (jnp.arange(owners, dtype=jnp.int32)[:, None] == owner[None, :]).astype(BF16)
    by_lane = (interface_slot % lanes)[:, None] == lane_number[None, :]
    parts = jnp.concatenate(
        [
            jnp.where(by_lane, (number // lanes)[:, None], 0),
            jnp.where(by_lane, (number % lanes)[:, None], 0),
        ],
        axis=1,
    ).astype(BF16)
    found = jnp.dot(by_owner, parts, preferred_element_type=F32).astype(jnp.int32)
    dof_blocks, dof_lanes = found[:, :lanes], found[:, lanes:]
    by_block = (
        jnp.arange(slabs * width, dtype=jnp.int32)[:, None] == (surface_local // lanes)[None, :]
    ).astype(BF16)
    marks = jnp.where(
        (surface_local % lanes)[:, None] == lane_number[None, :],
        jnp.arange(1, surface_local.shape[0] + 1, dtype=jnp.int32)[:, None],
        0,
    ).astype(BF16)
    inverse = (
        jnp.dot(by_block, marks, preferred_element_type=F32)
        .astype(jnp.int32)
        .reshape(slabs, width, lanes)
    )

    across_edge = passed_along(across_weight[-1:, :], SEC_CLU, 1)
    across_lower = jnp.concatenate([across_edge, across_weight[:-1, :]], axis=0)
    along_edge = passed_along(along_weight[:, -1:], BLK, 1)
    along_lower = jnp.concatenate([along_edge, along_weight[:, :-1]], axis=1)
    tile = jnp.arange(width, dtype=jnp.int32)[None, :]
    weights = jnp.stack(
        [
            block_weight,
            across_weight,
            across_lower,
            jnp.where(tile < width - 1, along_weight, 0.0),
            jnp.where(tile > 0, along_lower, 0.0),
            jnp.where(tile == width - 1, along_weight, 0.0),
            jnp.where(tile == 0, along_lower, 0.0),
        ]
    )
    weights = jnp.broadcast_to(weights[..., None], (*weights.shape, lanes))
    matrices = jnp.stack(
        [block_stiffness, across_matrix, across_matrix.T, along_matrix, along_matrix.T]
    )

    half_columns = clu_count
    slots_shape = (owners, cases, lanes)
    forward_inputs = (rows_local, columns_local, live_local, half_local)
    forward_inputs += (slot_lanes, slot_blocks, blocks_local)
    forward_specs = [SMEM] * 4 + [VMEM] * 3
    solution = None
    residual = right_side
    direction = right_side
    slot_residual = slot_direction = sums = None
    for iteration in range(ITERS):
        first = iteration == 0
        last = iteration + 1 == ITERS
        deep = 2 * cases if last else cases
        scratch = [
            pltpu.VMEM((slot_count // lanes, deep, lanes), BF16),
            pltpu.VMEM((2 * half_columns, deep, lanes), F32),
        ]
        halves = (like((half_columns, deep, lanes)),) * 2
        if first:
            slot_direction, keep, send = pl.pallas_call(
                functools.partial(forward_kernel, True, False),
                out_shape=(like(slots_shape), *halves),
                in_specs=forward_specs + [VMEM] * 2,
                scratch_shapes=scratch,
                name="forward_first",
            )(*forward_inputs, mine, other)
            slot_residual = slot_direction
        elif not last:
            slot_residual, slot_direction, keep, send = pl.pallas_call(
                functools.partial(forward_kernel, False, False),
                out_shape=(like(slots_shape), like(slots_shape), *halves),
                in_specs=forward_specs + [VMEM] * 5,
                scratch_shapes=scratch,
                name="forward",
            )(*forward_inputs, slot_residual, slot_direction, mine, other, sums)
        else:
            keep, send = pl.pallas_call(
                functools.partial(forward_kernel, False, True),
                out_shape=halves,
                in_specs=forward_specs + [VMEM] * 5,
                scratch_shapes=[pltpu.VMEM(slots_shape, F32)] + scratch,
                name="forward_last",
            )(*forward_inputs, slot_residual, slot_direction, mine, other, sums)
        column_pieces = exchanged(keep + partner(send), CLU)

        if not first:
            inputs = (sums, own, inverse, image, residual, direction)
            if iteration > 1:
                inputs += (solution,)
            solution, residual, direction = pl.pallas_call(
                functools.partial(update_kernel, iteration == 1),
                out_shape=(like(field),) * 3,
                scratch_shapes=[pltpu.VMEM((cases, lanes), F32)] * 2,
                name="update",
            )(*inputs)
        rounded_before = direction[:, -1].astype(BF16)
        rounded_after = direction[:, 0].astype(BF16)
        rounded_left = direction[:, :, -1].astype(BF16)
        rounded_right = direction[:, :, 0].astype(BF16)
        before = passed_along(rounded_before, SEC_CLU, 1)
        after = passed_along(rounded_after, SEC_CLU, -1)
        left = passed_along(rounded_left, BLK, 1)
        right = passed_along(rounded_right, BLK, -1)
        stiffness_inputs = (direction, residual, before, after, left, right)
        stiffness_inputs += (weights, matrices, surface)
        edges = [pltpu.VMEM((cases, slabs, lanes), F32)] * 2
        edges += [pltpu.VMEM((4, cases, lanes), F32)]
        if last:
            dots = pl.pallas_call(
                functools.partial(stiffness_kernel, False),
                out_shape=like((cases, lanes)),
                scratch_shapes=[pltpu.VMEM(field, F32)] + edges,
                name="stiffness_last",
            )(*stiffness_inputs)
            rows = pl.pallas_call(
                last_sums_kernel,
                out_shape=like((all_count, 1, lanes)),
                name="last_sums",
            )(column_pieces, dots)
            totals = exchanged(rows, ALL)
            return pl.pallas_call(
                final_kernel,
                out_shape=like(field),
                scratch_shapes=[pltpu.VMEM((cases, lanes), F32)],
                name="final",
            )(totals, direction, solution)
        image, image_trace, dots = pl.pallas_call(
            functools.partial(stiffness_kernel, True),
            out_shape=(like(field), like((cases, lanes)), like((cases, lanes))),
            scratch_shapes=edges,
            name="stiffness",
        )(*stiffness_inputs)

        z_low = column_pieces.sum(axis=0).astype(BF16)
        low_mine = exchanged(jnp.broadcast_to(z_low, (clu_count, *z_low.shape)), CLU)
        low_other = partner(low_mine)
        keep, send = pl.pallas_call(
            backward_kernel,
            out_shape=(like((blk_count, cases, lanes)),) * 2,
            in_specs=[SMEM] * 4 + [VMEM] * 5,
            scratch_shapes=[
                pltpu.VMEM((2 * half_columns, cases, lanes), BF16),
                pltpu.VMEM((slot_count // lanes, cases, lanes), F32),
            ],
            name="backward",
        )(
            rows_local,
            columns_local,
            live_local,
            half_local,
            dof_lanes,
            dof_blocks,
            blocks_local,
            low_mine,
            low_other,
        )
        arrived = exchanged(keep + partner(send), BLK)
        payload, own = pl.pallas_call(
            own_kernel,
            out_shape=(like((blk_count, cases + 8, lanes)), like((cases, lanes))),
            in_specs=[SMEM] + [VMEM] * 5,
            name="own",
        )(place_local, arrived, image_trace, dots, slot_residual, slot_direction)
        mine = exchanged(payload, BLK)
        other = partner(mine)
        range_sums = pl.pallas_call(
            range_sum_kernel,
            out_shape=like((clu_count, cases, lanes)),
            name="range_sums",
        )(mine, other)
        sums = exchanged(range_sums, CLU)


def solution(mesh):
    finer = Mesh(
        mesh.devices.reshape(mesh.shape["sec"], 4, 2, 2, 8),
        ("sec", "clu_0", "clu_1", "blk_0", "blk_1"),
    )
    placed = (
        P(None, SEC_CLU, BLK, None),
        P(SEC_CLU, BLK),
        P(SEC_CLU, BLK),
        P(SEC_CLU, BLK),
        P(),
        P(),
        P(),
        P("sec", CLU, BLK, None, None),
        P("sec", CLU, BLK),
        P("sec", CLU, BLK),
        P("sec", CLU, BLK),
        P("sec", CLU, BLK),
        P(CLU),
    )
    return jax.shard_map(
        shards, mesh=finer, in_specs=placed, out_specs=P(None, SEC_CLU, BLK, None), check_vma=False
    )
```

```python
import functools

import jax
import jax.numpy as jnp
from jax import lax
from jax.experimental import pallas as pl
from jax.experimental.pallas import tpu as pltpu
from jax.sharding import Mesh
from jax.sharding import PartitionSpec as P

ITERS = 3
ALL = ("sec", "clu_0", "clu_1", "blk_0", "blk_1")
SEC_CLU = ("sec", "clu_0", "clu_1")
BLK = ("blk_0", "blk_1")
CLU = ("clu_0", "clu_1")
F32 = jnp.float32
BF16 = jnp.bfloat16
SMEM = pl.BlockSpec(memory_space=pltpu.SMEM)
VMEM = pl.BlockSpec(memory_space=pltpu.VMEM)
LIMIT = 24 * 1024 * 1024


def passed_along(value, axis, by):
    count = lax.axis_size(axis)
    pairs = [(i, i + by) for i in range(count) if 0 <= i + by < count]
    return lax.ppermute(value, axis, pairs)


def partner(value):
    return lax.ppermute(value, "sec", [(0, 1), (1, 0)])


def exchanged(pieces, axes):
    return lax.all_to_all(pieces, axes, split_axis=0, concat_axis=0, tiled=True)


class near:
    def __init__(self, value):
        self.value = value


def kernel(body, outs, inputs, scratch=(), scalars=0):
    inputs = [
        pltpu.with_memory_space_constraint(x.value, pltpu.VMEM)
        if isinstance(x, near)
        else x
        if i < scalars
        else pltpu.with_memory_space_constraint(x, pltpu.HBM)
        for i, x in enumerate(inputs)
    ]
    return pl.pallas_call(
        body,
        out_shape=outs,
        in_specs=[SMEM] * scalars + [pl.BlockSpec()] * (len(inputs) - scalars),
        scratch_shapes=list(scratch),
        compiler_params=pltpu.CompilerParams(vmem_limit_bytes=LIMIT),
    )(*inputs)


def lanes_taken(rows, index):
    return jnp.take_along_axis(rows, index, axis=1)


def like(shape, dtype=F32):
    return pltpu.HBM(shape, dtype)


def kept(shape, dtype=F32):
    return pltpu.VMEM(shape, dtype)


def lane_iota(shape):
    return lax.broadcasted_iota(jnp.int32, shape, len(shape) - 1)


def row_iota(shape):
    return lax.broadcasted_iota(jnp.int32, shape, len(shape) - 2)


def column_to_row(column, at):
    cases = column.shape[0]
    shape = (cases, 128)
    here = lane_iota(shape) == row_iota(shape) + at
    return jnp.sum(jnp.where(here, column, 0.0), axis=0, keepdims=True)


def row_to_column(row, at, cases):
    shape = (cases, 128)
    here = lane_iota(shape) == row_iota(shape) + at
    return jnp.sum(jnp.where(here, row, 0.0), axis=1, keepdims=True)


def trace_of(ref, case, lane_index, block_index):
    slabs, width = ref.shape[1], ref.shape[2]
    sub = row_iota((width, 128))
    total = jnp.zeros((width, 128), F32)
    for a in range(slabs):
        picked = lanes_taken(ref[case, a], lane_index)
        total = jnp.where(block_index == a * width + sub, picked, total)
    return jnp.sum(total, axis=0, keepdims=True)


def edges_stored(case, a, value, slabs, edge_refs):
    before_ref, after_ref, left_ref, right_ref = edge_refs
    if a == slabs - 1:
        before_ref[case] = value
    if a == 0:
        after_ref[case] = value
    left_ref[case, a : a + 1, :] = value[-1:, :]
    right_ref[case, a : a + 1, :] = value[:1, :]


def edge_outputs(cases, slabs, width, lanes, make):
    return (make((cases, width, lanes)),) * 2 + (make((cases, slabs, lanes)),) * 2


def first_trace_kernel(field_ref, surface_ref, out_ref, *edge_refs):
    slabs = field_ref.shape[1]
    copies = out_ref.shape[0]
    lane_index = jnp.broadcast_to(surface_ref[0:1, :], (8, 128))
    block_index = jnp.broadcast_to(surface_ref[1:2, :], (8, 128))

    def step(case, carry):
        row = trace_of(field_ref, case, lane_index, block_index)
        out_ref[0, pl.ds(case, 1), :] = row
        for a in range(slabs):
            edges_stored(case, a, field_ref[case, a], slabs, edge_refs)
        return carry

    lax.fori_loop(0, field_ref.shape[0], step, 0, unroll=4)
    value = out_ref[0]
    for i in range(1, copies):
        out_ref[i] = value


def permuted_block(source_ref, lanes_ref, blocks_ref, d):
    count, cases = source_ref.shape[0], source_ref.shape[1]
    lane_index = jnp.broadcast_to(lanes_ref[pl.ds(d, 1), :], (8, 128))
    block_index = jnp.broadcast_to(blocks_ref[pl.ds(d, 1), :], (8, 128))
    groups = cases // 8
    totals = [jnp.zeros((8, 128), F32) for _ in range(groups)]
    for b in range(count):
        here = block_index == b
        for g in range(groups):
            picked = lanes_taken(source_ref[b, 8 * g : 8 * g + 8, :], lane_index)
            totals[g] = jnp.where(here, picked, totals[g])
    return totals


def scalars_of(pieces_ref):
    return jnp.sum(pieces_ref[...], axis=0)


def alpha_beta(sums):
    norm = sums[:, 0:1]
    curvature = sums[:, 1:2]
    alpha = norm / curvature
    following = norm - 2.0 * alpha * sums[:, 2:3] + alpha * alpha * sums[:, 3:4]
    beta = jnp.maximum(following, 0.0) / norm
    return alpha, beta


def forward_kernel(first, last, *refs):
    refs = list(refs)
    pairs_ref, lanes_ref, blocks_ref, boundary_ref = refs[:4]
    refs = refs[4:]
    if first:
        mine_ref, other_ref, direction_ref, slots_ref, keep_ref, send_ref, low_ref = refs[:7]
        rest = refs[7:]
        count = mine_ref.shape[0]
        direction_ref[:count] = mine_ref[...]
        direction_ref[count:] = other_ref[...]
    else:
        old_residual_ref, old_direction_ref, mine_ref, other_ref, sums_ref = refs[:5]
        if last:
            keep_ref, send_ref, direction_ref, low_ref = refs[5:9]
            rest = refs[9:]
        else:
            residual_ref, direction_ref, slots_ref, keep_ref, send_ref, low_ref = refs[5:11]
            rest = refs[11:]
        cases = old_direction_ref.shape[1]
        count = mine_ref.shape[0]
        alpha, beta = alpha_beta(scalars_of(sums_ref))
        alpha = jnp.broadcast_to(alpha, (cases, 128))
        beta = jnp.broadcast_to(beta, (cases, 128))
        for half, image_ref in ((0, mine_ref), (1, other_ref)):
            for i in range(count):
                b = half * count + i
                residual = old_residual_ref[b] - alpha * image_ref[i, :cases, :]
                if not last:
                    residual_ref[b] = residual
                direction_ref[b] = residual + beta * old_direction_ref[b]
    cases = direction_ref.shape[1]
    if not last:
        place = pairs_ref[3, 0]
        slots_ref[0] = direction_ref[place] if first else residual_ref[place]
        slots_ref[1] = direction_ref[place]

    def step(d, carry):
        totals = permuted_block(direction_ref, lanes_ref, blocks_ref, d)
        value = jnp.concatenate(totals, axis=0)
        low = value.astype(BF16)
        if last:
            left = value - low.astype(F32)
            second = left.astype(BF16)
            low_ref[d] = jnp.concatenate([low, second], axis=0)
        else:
            low_ref[d] = low
        return carry

    lax.fori_loop(0, direction_ref.shape[0], step, 0, unroll=2)
    half_count = keep_ref.shape[0]
    sums_scratch = rest[0]
    sums_scratch[...] = jnp.zeros(sums_scratch.shape, F32)
    live = pairs_ref[2, 0]
    for p in range(boundary_ref.shape[0]):
        product = jnp.dot(low_ref[pairs_ref[0, p]], boundary_ref[p], preferred_element_type=F32)
        product = jnp.where(p < live, product, 0.0)
        sums_scratch[pairs_ref[1, p]] += product
    keep_ref[...] = sums_scratch[:half_count]
    send_ref[...] = sums_scratch[half_count:]


def backward_kernel(
    pairs_ref,
    lanes_ref,
    blocks_ref,
    boundary_ref,
    mine_ref,
    other_ref,
    keep_ref,
    send_ref,
    low_ref,
    rows_scratch,
):
    half_count = mine_ref.shape[0]
    low_ref[:half_count] = mine_ref[...]
    low_ref[half_count:] = other_ref[...]
    rows_scratch[...] = jnp.zeros(rows_scratch.shape, F32)
    live = pairs_ref[2, 0]
    for p in range(boundary_ref.shape[0]):
        product = lax.dot_general(
            low_ref[pairs_ref[1, p]],
            boundary_ref[p],
            (((1,), (1,)), ((), ())),
            preferred_element_type=F32,
        )
        product = jnp.where(p < live, product, 0.0)
        rows_scratch[pairs_ref[0, p]] += product
    count = keep_ref.shape[0]
    for at, out_ref in ((0, keep_ref), (count, send_ref)):

        def step(d, carry, at=at, out_ref=out_ref):
            totals = permuted_block(rows_scratch, lanes_ref, blocks_ref, at + d)
            for g, total in enumerate(totals):
                out_ref[d, 8 * g : 8 * g + 8, :] = total
            return carry

        lax.fori_loop(0, count, step, 0, unroll=2)


def low_kernel(pieces_ref, out_ref):
    low = jnp.sum(pieces_ref[...], axis=0).astype(BF16)
    for i in range(out_ref.shape[0]):
        out_ref[i] = low


def stiffness(direction_ref, residual_ref, halo_refs, given_refs, out_refs, scratch_refs):
    before_ref, after_ref, left_ref, right_ref = halo_refs
    weights_ref, matrices_ref, surface_ref = given_refs
    image_ref, dots_ref, *more_refs = out_refs
    low_ref, high_ref, sums_ref = scratch_refs
    want_trace = len(more_refs) > 0
    cases, slabs, width = direction_ref.shape[:3]
    rows = cases * width

    def product(value, which):
        return jnp.dot(
            value.reshape(rows, 128).astype(BF16),
            matrices_ref[which],
            preferred_element_type=F32,
        ).reshape(cases, width, 128)

    def taken(a):
        if a < 0:
            return before_ref[...]
        if a == slabs:
            return after_ref[...]
        return direction_ref[:, a]

    high_ref[...] = product(right_ref[...], 3)
    low_ref[...] = product(left_ref[...], 4)
    for a in range(slabs):
        own = taken(a)
        result = weights_ref[0, a][None] * product(own, 0)
        result = result - weights_ref[1, a][None] * product(taken(a + 1), 1)
        result = result - weights_ref[2, a][None] * product(taken(a - 1), 2)
        result = result - weights_ref[3, a][None] * pltpu.roll(product(own, 3), width - 1, 1)
        result = result - weights_ref[4, a][None] * pltpu.roll(product(own, 4), 1, 1)
        result = result - weights_ref[5, a][None] * high_ref[:, a : a + 1, :]
        result = result - weights_ref[6, a][None] * low_ref[:, a : a + 1, :]
        image_ref[:, a] = result
    lane_index = jnp.broadcast_to(surface_ref[0:1, :], (8, 128))
    block_index = jnp.broadcast_to(surface_ref[1:2, :], (8, 128))

    def step(case, carry):
        r = residual_ref[case]
        d = direction_ref[case]
        q = image_ref[case]
        pairs = ((r, r), (d, q), (r, q), (q, q)) if want_trace else ((r, r), (d, q))
        for i, (one, two) in enumerate(pairs):
            sums_ref[i, pl.ds(case, 1), :] = jnp.sum(
                jnp.sum(one * two, axis=0), axis=0, keepdims=True
            )
        if want_trace:
            more_refs[0][pl.ds(case, 1), :] = trace_of(image_ref, case, lane_index, block_index)
            for a in range(slabs):
                edges_stored(case, a, image_ref[case, a], slabs, more_refs[1:])
        return carry

    lax.fori_loop(0, cases, step, 0, unroll=4)
    lane = lane_iota((cases, 128))
    dots = jnp.zeros((cases, 128), F32)
    for i in range(4 if want_trace else 2):
        dots = jnp.where(lane == i, jnp.sum(sums_ref[i], axis=1, keepdims=True), dots)
    dots_ref[...] = dots


def first_stiffness_kernel(direction_ref, *refs):
    stiffness(direction_ref, direction_ref, refs[:4], refs[4:7], refs[7:14], refs[14:])


def field_kernel(first, last, *refs):
    refs = list(refs)

    def take(n):
        taken = refs[:n]
        del refs[:n]
        return taken

    sums_ref, own_ref, inverse_ref, image_ref, residual_ref, direction_ref = take(6)
    solution_ref = None if first else take(1)[0]
    halo_image_refs, halo_residual_refs, halo_direction_refs = take(4), take(4), take(4)
    given_refs = take(3)
    new_solution_ref, new_direction_ref = take(2)
    if last:
        (dots_ref,) = take(1)
        new_residual_ref, new_image_ref = take(2)
        new_halo_direction_refs = take(4)
        new_halo_residual_refs = None
        out_refs = (new_image_ref, dots_ref)
    else:
        (new_residual_ref,) = take(1)
        new_halo_residual_refs, new_halo_direction_refs = take(4), take(4)
        out_refs = take(7)
    alpha_ref, beta_ref = take(2)
    cases, slabs, width = direction_ref.shape[:3]
    alpha, beta = alpha_beta(scalars_of(sums_ref))
    alpha_ref[...] = jnp.broadcast_to(alpha, (cases, 128))
    beta_ref[...] = jnp.broadcast_to(beta, (cases, 128))

    def step(case, carry):
        alpha = jnp.broadcast_to(alpha_ref[pl.ds(case, 1), :], (width, 128))
        beta = jnp.broadcast_to(beta_ref[pl.ds(case, 1), :], (width, 128))
        own = jnp.broadcast_to(own_ref[pl.ds(case, 1), :], (width, 128))
        for i in range(4):
            r = halo_residual_refs[i][case] - alpha * halo_image_refs[i][case]
            if not last:
                new_halo_residual_refs[i][case] = r
            new_halo_direction_refs[i][case] = r + beta * halo_direction_refs[i][case]
        for a in range(slabs):
            slot = inverse_ref[a]
            there = slot > 0
            extra = lanes_taken(own, jnp.where(there, slot - 1, 0))
            image = image_ref[case, a] + jnp.where(there, extra, 0.0)
            d = direction_ref[case, a]
            r = residual_ref[case, a] - alpha * image
            new_residual_ref[case, a] = r
            moved = alpha * d
            if solution_ref is not None:
                moved = solution_ref[case, a] + moved
            new_solution_ref[case, a] = moved
            new_direction_ref[case, a] = r + beta * d
        return carry

    lax.fori_loop(0, cases, step, 0, unroll=4)
    stiffness(
        new_direction_ref, new_residual_ref, new_halo_direction_refs, given_refs, out_refs, refs
    )


def own_kernel(arrived_ref, trace_ref, dots_ref, slots_ref, inverse_ref, *refs):
    edge_refs, (out_ref, own_ref), new_edge_refs = refs[:4], refs[4:6], refs[6:]
    copies, cases = out_ref.shape[0], trace_ref.shape[0]
    slabs, width = inverse_ref.shape[:2]
    y = jnp.sum(arrived_ref[...], axis=0)
    own_ref[...] = y
    trace = trace_ref[...]
    r = slots_ref[0]
    d = slots_ref[1]
    dots = dots_ref[...]
    terms = (None, d * y, r * y, (2.0 * trace + y) * y)
    row = jnp.zeros((1, 128), F32)
    for i, term in enumerate(terms):
        column = dots[:, i : i + 1]
        if term is not None:
            column = column + jnp.sum(term, axis=1, keepdims=True)
        row = row + column_to_row(column, i * cases)
    image = trace + y
    row8 = jnp.broadcast_to(row, (8, 128))
    for i in range(copies):
        out_ref[i, :cases, :] = image
        out_ref[i, cases:, :] = row8
    sides = (
        inverse_ref[slabs - 1],
        inverse_ref[0],
        jnp.concatenate([inverse_ref[a, width - 1 :, :] for a in range(slabs)], axis=0),
        jnp.concatenate([inverse_ref[a, :1, :] for a in range(slabs)], axis=0),
    )

    def step(case, carry):
        values = jnp.broadcast_to(own_ref[pl.ds(case, 1), :], (8, 128))
        for slot, edge_ref, new_edge_ref in zip(sides, edge_refs, new_edge_refs):
            there = slot > 0
            extra = lanes_taken(values, jnp.where(there, slot - 1, 0))
            new_edge_ref[case] = edge_ref[case] + jnp.where(there, extra, 0.0)
        return carry

    lax.fori_loop(0, cases, step, 0, unroll=4)


def range_sum_kernel(mine_ref, other_ref, out_ref):
    copies, cases = out_ref.shape[0], out_ref.shape[1]
    row = jnp.sum(mine_ref[:, cases : cases + 8, :], axis=0) + jnp.sum(
        other_ref[:, cases : cases + 8, :], axis=0
    )
    row = row[0:1, :]
    lane = lane_iota((cases, 128))
    sums = jnp.zeros((cases, 128), F32)
    for i in range(4):
        sums = jnp.where(lane == i, row_to_column(row, i * cases, cases), sums)
    for i in range(copies):
        out_ref[i] = sums


def last_sums_kernel(arrived_ref, dots_ref, out_ref):
    copies = out_ref.shape[0]
    cases = dots_ref.shape[0]
    total = jnp.sum(arrived_ref[...], axis=0)
    z = total[:cases]
    rest = total[cases:]
    low = z.astype(BF16).astype(F32)
    dots = dots_ref[...]
    curvature = dots[:, 1:2] + jnp.sum((z + rest) * low, axis=1, keepdims=True)
    row = column_to_row(dots[:, 0:1], 0) + column_to_row(curvature, cases)
    out_ref[...] = jnp.broadcast_to(row[None], (copies, 1, 128))


def final_kernel(sums_ref, direction_ref, solution_ref, out_ref, alpha_ref):
    cases, slabs, width = direction_ref.shape[:3]
    row = jnp.sum(sums_ref[...], axis=0)
    norm = row_to_column(row, 0, cases)
    curvature = row_to_column(row, cases, cases)
    alpha_ref[...] = jnp.broadcast_to(norm / curvature, (cases, 128))

    def step(case, carry):
        alpha = jnp.broadcast_to(alpha_ref[pl.ds(case, 1), :], (width, 128))
        for a in range(slabs):
            out_ref[case, a] = solution_ref[case, a] + alpha * direction_ref[case, a]
        return carry

    lax.fori_loop(0, cases, step, 0, unroll=2)


def shards(
    right_side,
    block_weight,
    across_weight,
    along_weight,
    block_stiffness,
    across_matrix,
    along_matrix,
    boundary_blocks,
    block_rows,
    block_columns,
    live_pairs,
    surface_index,
    interface_slot,
):
    cases, slabs, width, lanes = right_side.shape
    field = right_side.shape
    rows_local = block_rows[0, 0]
    columns_local = block_columns[0, 0]
    blocks_local = boundary_blocks[0, 0]
    live_local = live_pairs[0, 0]
    surface_local = surface_index[0, 0]
    half = lax.axis_index("sec").astype(jnp.int32)
    place = lax.axis_index(BLK).astype(jnp.int32)
    blk_count = lax.axis_size(BLK)
    clu_count = lax.axis_size(CLU)
    owners = 2 * blk_count
    all_count = owners * clu_count
    slot_count = interface_slot.shape[0]
    surface = jnp.stack([surface_local % lanes, surface_local // lanes])

    def edges_by(make):
        return edge_outputs(cases, slabs, width, lanes, make)

    def sent(edges):
        before = passed_along(edges[0], SEC_CLU, 1)
        after = passed_along(edges[1], SEC_CLU, -1)
        left = passed_along(edges[2], BLK, 1)
        right = passed_along(edges[3], BLK, -1)
        return before, after, left, right

    trace, *edges = kernel(
        first_trace_kernel,
        (kept((blk_count, cases, lanes)), *edges_by(kept)),
        (right_side, surface),
    )
    mine = exchanged(trace, BLK)
    other = partner(mine)

    owner = (interface_slot // lanes) ^ (half * blk_count)
    slot_blocks = owner.reshape(slot_count // lanes, lanes)
    slot_lanes = (interface_slot % lanes).reshape(slot_count // lanes, lanes)
    number = jnp.arange(slot_count, dtype=jnp.int32)
    lane_number = jnp.arange(lanes, dtype=jnp.int32)
    by_owner = (jnp.arange(owners, dtype=jnp.int32)[:, None] == owner[None, :]).astype(BF16)
    by_lane = (interface_slot % lanes)[:, None] == lane_number[None, :]
    parts = jnp.concatenate(
        [
            jnp.where(by_lane, (number // lanes)[:, None], 0),
            jnp.where(by_lane, (number % lanes)[:, None], 0),
        ],
        axis=1,
    ).astype(BF16)
    found = jnp.dot(by_owner, parts, preferred_element_type=F32).astype(jnp.int32)
    dof_blocks, dof_lanes = found[:, :lanes], found[:, lanes:]
    by_block = (
        jnp.arange(slabs * width, dtype=jnp.int32)[:, None] == (surface_local // lanes)[None, :]
    ).astype(BF16)
    marks = jnp.where(
        (surface_local % lanes)[:, None] == lane_number[None, :],
        jnp.arange(1, surface_local.shape[0] + 1, dtype=jnp.int32)[:, None],
        0,
    ).astype(BF16)
    inverse = (
        jnp.dot(by_block, marks, preferred_element_type=F32)
        .astype(jnp.int32)
        .reshape(slabs, width, lanes)
    )

    across_edge = passed_along(across_weight[-1:, :], SEC_CLU, 1)
    across_lower = jnp.concatenate([across_edge, across_weight[:-1, :]], axis=0)
    along_edge = passed_along(along_weight[:, -1:], BLK, 1)
    along_lower = jnp.concatenate([along_edge, along_weight[:, :-1]], axis=1)
    tile = jnp.arange(width, dtype=jnp.int32)[None, :]
    weights = jnp.stack(
        [
            block_weight,
            across_weight,
            across_lower,
            jnp.where(tile < width - 1, along_weight, 0.0),
            jnp.where(tile > 0, along_lower, 0.0),
            jnp.where(tile == width - 1, along_weight, 0.0),
            jnp.where(tile == 0, along_lower, 0.0),
        ]
    )
    weights = jnp.broadcast_to(weights[..., None], (*weights.shape, lanes))
    matrices = jnp.stack(
        [block_stiffness, across_matrix, across_matrix.T, along_matrix, along_matrix.T]
    )

    half_columns = clu_count
    slots_shape = (owners, cases, lanes)
    pairs = jnp.stack(
        [
            rows_local,
            columns_local ^ (half * half_columns),
            jnp.broadcast_to(live_local, rows_local.shape),
            jnp.broadcast_to(place, rows_local.shape),
        ]
    )
    forward_inputs = (pairs, slot_lanes, slot_blocks, near(blocks_local))
    given = (weights, matrices, surface)
    edge_kept, edge_like = edges_by(kept), edges_by(like)
    own_slots_shape = like((2, cases, lanes))
    image_outputs = (like(field), like((cases, lanes)), like((cases, lanes)), *edge_like)
    stiffness_scratch = [pltpu.VMEM((cases, slabs, lanes), F32)] * 2
    stiffness_scratch += [pltpu.VMEM((4, cases, lanes), F32)]
    field_scratch = [pltpu.VMEM((cases, lanes), F32)] * 2 + stiffness_scratch
    solution = None
    residual = right_side
    direction = right_side
    slot_residual = slot_direction = sums = None
    for iteration in range(ITERS):
        first = iteration == 0
        last = iteration + 1 == ITERS
        deep = 2 * cases if last else cases
        scratch = [
            pltpu.VMEM((slot_count // lanes, deep, lanes), BF16),
            pltpu.VMEM((2 * half_columns, deep, lanes), F32),
        ]
        halves = (kept((half_columns, deep, lanes)),) * 2
        if first:
            slot_direction, own_slots, keep, send = kernel(
                functools.partial(forward_kernel, True, False),
                (like(slots_shape), own_slots_shape, *halves),
                (*forward_inputs, near(mine), near(other)),
                scratch,
                1,
            )
            slot_residual = slot_direction
        else:
            inputs = (*forward_inputs, slot_residual, slot_direction)
            inputs += (near(mine), near(other), near(sums))
            if last:
                keep, send = kernel(
                    functools.partial(forward_kernel, False, True),
                    halves,
                    inputs,
                    [pltpu.VMEM(slots_shape, F32)] + scratch,
                    1,
                )
            else:
                slot_residual, slot_direction, own_slots, keep, send = kernel(
                    functools.partial(forward_kernel, False, False),
                    (like(slots_shape), like(slots_shape), own_slots_shape, *halves),
                    inputs,
                    scratch,
                    1,
                )
        pieces = keep + partner(send)
        column_pieces = exchanged(pieces, CLU)

        if first:
            halo_residual = halo_direction = sent(edges)
            image, dots, image_trace, *edges = kernel(
                first_stiffness_kernel,
                image_outputs,
                (right_side, *halo_direction, *given),
                stiffness_scratch,
            )
        else:
            inputs = (sums, own, inverse, image, residual, direction)
            if iteration > 1:
                inputs += (solution,)
            inputs += (*halo_image, *halo_residual, *halo_direction, *given)
            if last:
                solution, direction, dots = kernel(
                    functools.partial(field_kernel, iteration == 1, True),
                    (like(field), like(field), like((cases, lanes))),
                    inputs,
                    [pltpu.VMEM(field, F32)] * 2
                    + [pltpu.VMEM(edge.shape, F32) for edge in halo_image]
                    + field_scratch,
                )
            else:
                outs = kernel(
                    functools.partial(field_kernel, iteration == 1, False),
                    (like(field),) * 3 + edge_like * 2 + image_outputs,
                    inputs,
                    field_scratch,
                )
                solution, direction, residual = outs[:3]
                halo_residual, halo_direction = outs[3:7], outs[7:11]
                image, dots, image_trace, *edges = outs[11:]
        if last:
            rows = kernel(
                last_sums_kernel,
                kept((all_count, 1, lanes)),
                (near(column_pieces), dots),
            )
            totals = exchanged(rows, ALL)
            return kernel(
                final_kernel,
                like(field),
                (near(totals), direction, solution),
                [pltpu.VMEM((cases, lanes), F32)],
            )

        z_low = kernel(
            low_kernel, kept((clu_count, cases, lanes), BF16), (near(column_pieces),)
        )
        low_mine = exchanged(z_low, CLU)
        low_other = partner(low_mine)
        keep, send = kernel(
            backward_kernel,
            (kept((blk_count, cases, lanes)),) * 2,
            (
                pairs,
                dof_lanes,
                dof_blocks,
                near(blocks_local),
                near(low_mine),
                near(low_other),
            ),
            [
                pltpu.VMEM((2 * half_columns, cases, lanes), BF16),
                pltpu.VMEM((slot_count // lanes, cases, lanes), F32),
            ],
            1,
        )
        row_pieces = keep + partner(send)
        arrived = exchanged(row_pieces, BLK)
        payload, own, *edges = kernel(
            own_kernel,
            (kept((blk_count, cases + 8, lanes)), like((cases, lanes)), *edge_kept),
            (near(arrived), image_trace, dots, own_slots, inverse, *edges),
        )
        mine = exchanged(payload, BLK)
        halo_image = sent(edges)
        other = partner(mine)
        range_sums = kernel(
            range_sum_kernel, kept((clu_count, cases, lanes)), (near(mine), near(other))
        )
        sums = exchanged(range_sums, CLU)


def solution(mesh):
    finer = Mesh(
        mesh.devices.reshape(mesh.shape["sec"], 4, 2, 2, 8),
        ("sec", "clu_0", "clu_1", "blk_0", "blk_1"),
    )
    placed = (
        P(None, SEC_CLU, BLK, None),
        P(SEC_CLU, BLK),
        P(SEC_CLU, BLK),
        P(SEC_CLU, BLK),
        P(),
        P(),
        P(),
        P("sec", CLU, BLK, None, None),
        P("sec", CLU, BLK),
        P("sec", CLU, BLK),
        P("sec", CLU, BLK),
        P("sec", CLU, BLK),
        P(CLU),
    )
    return jax.shard_map(
        shards, mesh=finer, in_specs=placed, out_specs=P(None, SEC_CLU, BLK, None), check_vma=False
    )
```

```python
import functools

import jax
import jax.numpy as jnp
from jax import lax
from jax.experimental import pallas as pl
from jax.experimental.pallas import tpu as pltpu
from jax.sharding import Mesh
from jax.sharding import PartitionSpec as P

ITERS = 3
ALL = ("sec", "clu_0", "clu_1", "blk_0", "blk_1")
SEC_CLU = ("sec", "clu_0", "clu_1")
BLK = ("blk_0", "blk_1")
CLU = ("clu_0", "clu_1")
F32 = jnp.float32
BF16 = jnp.bfloat16
SMEM = pl.BlockSpec(memory_space=pltpu.SMEM)
VMEM = pl.BlockSpec(memory_space=pltpu.VMEM)
LIMIT = 24 * 1024 * 1024


def passed_along(value, axis, by):
    count = lax.axis_size(axis)
    pairs = [(i, i + by) for i in range(count) if 0 <= i + by < count]
    return lax.ppermute(value, axis, pairs)


def partner(value):
    return lax.ppermute(value, "sec", [(0, 1), (1, 0)])


def exchanged(pieces, axes):
    return lax.all_to_all(pieces, axes, split_axis=0, concat_axis=0, tiled=True)


class near:
    def __init__(self, value):
        self.value = value


def kernel(body, outs, inputs, scratch=(), scalars=0):
    inputs = [
        pltpu.with_memory_space_constraint(x.value, pltpu.VMEM)
        if isinstance(x, near)
        else x
        if i < scalars
        else pltpu.with_memory_space_constraint(x, pltpu.HBM)
        for i, x in enumerate(inputs)
    ]
    return pl.pallas_call(
        body,
        out_shape=outs,
        in_specs=[SMEM] * scalars + [pl.BlockSpec()] * (len(inputs) - scalars),
        scratch_shapes=list(scratch),
        compiler_params=pltpu.CompilerParams(vmem_limit_bytes=LIMIT),
    )(*inputs)


def lanes_taken(rows, index):
    return jnp.take_along_axis(rows, index, axis=1)


def like(shape, dtype=F32):
    return pltpu.HBM(shape, dtype)


def kept(shape, dtype=F32):
    return pltpu.VMEM(shape, dtype)


def lane_iota(shape):
    return lax.broadcasted_iota(jnp.int32, shape, len(shape) - 1)


def row_iota(shape):
    return lax.broadcasted_iota(jnp.int32, shape, len(shape) - 2)


def column_to_row(column, at):
    cases = column.shape[0]
    shape = (cases, 128)
    here = lane_iota(shape) == row_iota(shape) + at
    return jnp.sum(jnp.where(here, column, 0.0), axis=0, keepdims=True)


def row_to_column(row, at, cases):
    shape = (cases, 128)
    here = lane_iota(shape) == row_iota(shape) + at
    return jnp.sum(jnp.where(here, row, 0.0), axis=1, keepdims=True)


def trace_of(ref, case, lane_index, block_index):
    slabs, width = ref.shape[1], ref.shape[2]
    sub = row_iota((width, 128))
    total = jnp.zeros((width, 128), F32)
    for a in range(slabs):
        picked = lanes_taken(ref[case, a], lane_index)
        total = jnp.where(block_index == a * width + sub, picked, total)
    return jnp.sum(total, axis=0, keepdims=True)


def edges_stored(case, a, value, slabs, edge_refs):
    before_ref, after_ref, left_ref, right_ref = edge_refs
    if a == slabs - 1:
        before_ref[case] = value
    if a == 0:
        after_ref[case] = value
    left_ref[case, a : a + 1, :] = value[-1:, :]
    right_ref[case, a : a + 1, :] = value[:1, :]


def edge_outputs(cases, slabs, width, lanes, make):
    return (make((cases, width, lanes)),) * 2 + (make((cases, slabs, lanes)),) * 2


def first_trace_kernel(field_ref, surface_ref, end_ref, out_ref, *edge_refs):
    cases, slabs = field_ref.shape[:2]
    copies = out_ref.shape[0]
    edge_refs[0][cases] = end_ref[0]
    edge_refs[2][cases] = end_ref[1]
    local = jnp.broadcast_to(surface_ref[...], (8, 128))
    lane_index, block_index = local & 127, local >> 7

    def step(case, carry):
        row = trace_of(field_ref, case, lane_index, block_index)
        out_ref[0, pl.ds(case, 1), :] = row
        for a in range(slabs):
            edges_stored(case, a, field_ref[case, a], slabs, edge_refs)
        return carry

    lax.fori_loop(0, field_ref.shape[0], step, 0, unroll=4)
    value = out_ref[0]
    for i in range(1, copies):
        out_ref[i] = value


def permuted_block(source_ref, lanes_ref, blocks_ref, d):
    count, cases = source_ref.shape[0], source_ref.shape[1]
    lane_index = jnp.broadcast_to(lanes_ref[pl.ds(d, 1), :], (8, 128))
    block_index = jnp.broadcast_to(blocks_ref[pl.ds(d, 1), :], (8, 128))
    groups = cases // 8
    totals = [jnp.zeros((8, 128), F32) for _ in range(groups)]
    for b in range(count):
        here = block_index == b
        for g in range(groups):
            picked = lanes_taken(source_ref[b, 8 * g : 8 * g + 8, :], lane_index)
            totals[g] = jnp.where(here, picked, totals[g])
    return totals


def alpha_beta(sums_ref, cases):
    row = jnp.sum(sums_ref[...], axis=0)
    norm, curvature, crossed, squared = (row_to_column(row, i * cases, cases) for i in range(4))
    alpha = norm / curvature
    following = norm - 2.0 * alpha * crossed + alpha * alpha * squared
    beta = jnp.maximum(following, 0.0) / norm
    return alpha, beta


def forward_kernel(first, last, *refs):
    refs = list(refs)
    pairs_ref, lanes_ref, blocks_ref, boundary_ref = refs[:4]
    refs = refs[4:]
    if first:
        mine_ref, other_ref, direction_ref, slots_ref, keep_ref, send_ref, low_ref = refs[:7]
        rest = refs[7:]
        count = mine_ref.shape[0]
        direction_ref[:count] = mine_ref[...]
        direction_ref[count:] = other_ref[...]
    else:
        old_residual_ref, old_direction_ref, mine_ref, other_ref, sums_ref = refs[:5]
        steps_ref, refs = refs[5], refs[6:]
        if last:
            keep_ref, send_ref, direction_ref, low_ref = refs[:4]
            rest = refs[4:]
        else:
            residual_ref, direction_ref, slots_ref, keep_ref, send_ref, low_ref = refs[:6]
            rest = refs[6:]
        cases = old_direction_ref.shape[1]
        count = mine_ref.shape[0]
        alpha, beta = alpha_beta(sums_ref, cases)
        alpha = jnp.broadcast_to(alpha, (cases, 128))
        beta = jnp.broadcast_to(beta, (cases, 128))
        steps_ref[0] = alpha
        steps_ref[1] = beta
        for half, image_ref in ((0, mine_ref), (1, other_ref)):
            for i in range(count):
                b = half * count + i
                residual = old_residual_ref[b] - alpha * image_ref[i, :cases, :]
                if not last:
                    residual_ref[b] = residual
                direction_ref[b] = residual + beta * old_direction_ref[b]
    cases = direction_ref.shape[1]
    if not last:
        place = pairs_ref[3, 0]
        slots_ref[0] = direction_ref[place] if first else residual_ref[place]
        slots_ref[1] = direction_ref[place]

    def step(d, carry):
        totals = permuted_block(direction_ref, lanes_ref, blocks_ref, d)
        value = jnp.concatenate(totals, axis=0)
        low = value.astype(BF16)
        if last:
            left = value - low.astype(F32)
            second = left.astype(BF16)
            low_ref[d] = jnp.concatenate([low, second], axis=0)
        else:
            low_ref[d] = low
        return carry

    lax.fori_loop(0, direction_ref.shape[0], step, 0, unroll=4)
    half_count = keep_ref.shape[0]
    sums_scratch = rest[0]
    sums_scratch[...] = jnp.zeros(sums_scratch.shape, F32)
    live = pairs_ref[2, 0]
    for p in range(boundary_ref.shape[0]):
        product = jnp.dot(low_ref[pairs_ref[0, p]], boundary_ref[p], preferred_element_type=F32)
        product = jnp.where(p < live, product, 0.0)
        sums_scratch[pairs_ref[1, p]] += product
    keep_ref[...] = sums_scratch[:half_count]
    send_ref[...] = sums_scratch[half_count:]


def backward_kernel(
    pairs_ref,
    lanes_ref,
    blocks_ref,
    boundary_ref,
    mine_ref,
    other_ref,
    keep_ref,
    send_ref,
    low_ref,
    rows_scratch,
):
    half_count = mine_ref.shape[0]
    low_ref[:half_count] = mine_ref[...]
    low_ref[half_count:] = other_ref[...]
    rows_scratch[...] = jnp.zeros(rows_scratch.shape, F32)
    live = pairs_ref[2, 0]
    for p in range(boundary_ref.shape[0]):
        product = lax.dot_general(
            low_ref[pairs_ref[1, p]],
            boundary_ref[p],
            (((1,), (1,)), ((), ())),
            preferred_element_type=F32,
        )
        product = jnp.where(p < live, product, 0.0)
        rows_scratch[pairs_ref[0, p]] += product
    count = keep_ref.shape[0]
    for at, out_ref in ((0, keep_ref), (count, send_ref)):

        def step(d, carry, at=at, out_ref=out_ref):
            totals = permuted_block(rows_scratch, lanes_ref, blocks_ref, at + d)
            for g, total in enumerate(totals):
                out_ref[d, 8 * g : 8 * g + 8, :] = total
            return carry

        lax.fori_loop(0, count, step, 0, unroll=4)


def low_kernel(pieces_ref, out_ref):
    low = jnp.sum(pieces_ref[...], axis=0).astype(BF16)
    for i in range(out_ref.shape[0]):
        out_ref[i] = low


def stiffness(direction_ref, residual_ref, halo_refs, given_refs, out_refs, scratch_refs):
    before_ref, after_ref, left_ref, right_ref = halo_refs
    weights_ref, matrices_ref, surface_ref = given_refs
    image_ref, dots_ref, *more_refs = out_refs
    low_ref, high_ref, sums_ref = scratch_refs
    want_trace = len(more_refs) > 0
    cases, slabs, width = direction_ref.shape[:3]
    rows = cases * width

    def product(value, which):
        return jnp.dot(
            value.reshape(rows, 128).astype(BF16),
            matrices_ref[which],
            preferred_element_type=F32,
        ).reshape(cases, width, 128)

    def taken(a):
        if a < 0:
            return before_ref[:cases]
        if a == slabs:
            return after_ref[...]
        return direction_ref[:, a]

    high_ref[...] = product(right_ref[...], 3)
    low_ref[...] = product(left_ref[:cases], 4)
    for a in range(slabs):
        own = taken(a)
        result = weights_ref[0, a][None] * product(own, 0)
        result = result - weights_ref[1, a][None] * product(taken(a + 1), 1)
        result = result - weights_ref[2, a][None] * product(taken(a - 1), 2)
        result = result - weights_ref[3, a][None] * pltpu.roll(product(own, 3), width - 1, 1)
        result = result - weights_ref[4, a][None] * pltpu.roll(product(own, 4), 1, 1)
        result = result - weights_ref[5, a][None] * high_ref[:, a : a + 1, :]
        result = result - weights_ref[6, a][None] * low_ref[:, a : a + 1, :]
        image_ref[:, a] = result
    local = jnp.broadcast_to(surface_ref[...], (8, 128))
    lane_index, block_index = local & 127, local >> 7

    def step(case, carry):
        r = residual_ref[case]
        d = direction_ref[case]
        q = image_ref[case]
        pairs = ((r, r), (d, q), (r, q), (q, q)) if want_trace else ((r, r), (d, q))
        for i, (one, two) in enumerate(pairs):
            sums_ref[i, pl.ds(case, 1), :] = jnp.sum(
                jnp.sum(one * two, axis=0), axis=0, keepdims=True
            )
        if want_trace:
            more_refs[0][pl.ds(case, 1), :] = trace_of(image_ref, case, lane_index, block_index)
            for a in range(slabs):
                edges_stored(case, a, image_ref[case, a], slabs, more_refs[1:])
        return carry

    lax.fori_loop(0, cases, step, 0, unroll=4)
    lane = lane_iota((cases, 128))
    dots = jnp.zeros((cases, 128), F32)
    for i in range(4 if want_trace else 2):
        dots = jnp.where(lane == i, jnp.sum(sums_ref[i], axis=1, keepdims=True), dots)
    dots_ref[...] = dots


def stiffness_kernel(same, direction_ref, *refs):
    residual_ref, refs = (direction_ref, refs) if same else (refs[0], refs[1:])
    stiffness(direction_ref, residual_ref, refs[:4], refs[4:7], refs[7:14], refs[14:])


def field_kernel(first, last, *refs):
    refs = list(refs)

    def take(n):
        taken = refs[:n]
        del refs[:n]
        return taken

    steps_ref, own_ref, inverse_ref, image_ref, residual_ref, direction_ref = take(6)
    solution_ref = None if first else take(1)[0]
    halo_image_refs, halo_residual_refs, halo_direction_refs = take(4), take(4), take(4)
    given_refs = take(3) if last else None
    new_solution_ref, new_direction_ref = take(2)
    if last:
        (dots_ref,) = take(1)
        new_residual_ref, new_image_ref = take(2)
        new_halo_direction_refs = take(4)
        new_halo_residual_refs = None
        out_refs = (new_image_ref, dots_ref)
    else:
        (new_residual_ref,) = take(1)
        new_halo_residual_refs, new_halo_direction_refs = take(4), take(4)
    cases, slabs, width = direction_ref.shape[:3]

    def step(case, carry):
        alpha = jnp.broadcast_to(steps_ref[0, pl.ds(case, 1), :], (width, 128))
        beta = jnp.broadcast_to(steps_ref[1, pl.ds(case, 1), :], (width, 128))
        own = jnp.broadcast_to(own_ref[pl.ds(case, 1), :], (width, 128))
        for i in range(4):
            r = halo_residual_refs[i][case] - alpha * halo_image_refs[i][case]
            if not last:
                new_halo_residual_refs[i][case] = r
            new_halo_direction_refs[i][case] = r + beta * halo_direction_refs[i][case]
        for a in range(slabs):
            slot = inverse_ref[a]
            there = slot > 0
            extra = lanes_taken(own, jnp.where(there, slot - 1, 0))
            image = image_ref[case, a] + jnp.where(there, extra, 0.0)
            d = direction_ref[case, a]
            r = residual_ref[case, a] - alpha * image
            new_residual_ref[case, a] = r
            moved = alpha * d
            if solution_ref is not None:
                moved = solution_ref[case, a] + moved
            new_solution_ref[case, a] = moved
            new_direction_ref[case, a] = r + beta * d
        return carry

    lax.fori_loop(0, cases, step, 0, unroll=4)
    if last:
        halo_refs = new_halo_direction_refs
        stiffness(new_direction_ref, new_residual_ref, halo_refs, given_refs, out_refs, refs)


def own_kernel(arrived_ref, trace_ref, dots_ref, slots_ref, out_ref, own_ref):
    copies, cases = out_ref.shape[0], trace_ref.shape[0]
    y = jnp.sum(arrived_ref[...], axis=0)
    own_ref[...] = y
    trace = trace_ref[...]
    r = slots_ref[0]
    d = slots_ref[1]
    dots = dots_ref[...]
    terms = (None, d * y, r * y, (2.0 * trace + y) * y)
    row = jnp.zeros((1, 128), F32)
    for i, term in enumerate(terms):
        column = dots[:, i : i + 1]
        if term is not None:
            column = column + jnp.sum(term, axis=1, keepdims=True)
        row = row + column_to_row(column, i * cases)
    image = trace + y
    rows = jnp.broadcast_to(row, (8, 128))
    for i in range(copies):
        out_ref[i, :cases, :] = image
        out_ref[i, cases:, :] = rows


def range_sum_kernel(cases, mine_ref, other_ref, out_ref):
    row = jnp.sum(mine_ref[:, cases:, :], axis=0) + jnp.sum(other_ref[:, cases:, :], axis=0)
    out_ref[...] = jnp.broadcast_to(row[0:1, :][None], out_ref.shape)


def edges_kernel(own_ref, inverse_ref, *refs):
    edge_refs, new_edge_refs = refs[:4], refs[4:]
    slabs, width = inverse_ref.shape[:2]
    sides = (
        inverse_ref[slabs - 1],
        inverse_ref[0],
        jnp.concatenate([inverse_ref[a, width - 1 :, :] for a in range(slabs)], axis=0),
        jnp.concatenate([inverse_ref[a, :1, :] for a in range(slabs)], axis=0),
    )

    def step(case, carry):
        values = jnp.broadcast_to(own_ref[pl.ds(case, 1), :], (8, 128))
        for slot, edge_ref, new_edge_ref in zip(sides, edge_refs, new_edge_refs):
            there = slot > 0
            extra = lanes_taken(values, jnp.where(there, slot - 1, 0))
            new_edge_ref[case] = edge_ref[case] + jnp.where(there, extra, 0.0)
        return carry

    lax.fori_loop(0, own_ref.shape[0], step, 0, unroll=4)


def last_sums_kernel(arrived_ref, dots_ref, out_ref):
    copies = out_ref.shape[0]
    cases = dots_ref.shape[0]
    total = jnp.sum(arrived_ref[...], axis=0)
    z = total[:cases]
    rest = total[cases:]
    low = z.astype(BF16).astype(F32)
    dots = dots_ref[...]
    curvature = dots[:, 1:2] + jnp.sum((z + rest) * low, axis=1, keepdims=True)
    row = column_to_row(dots[:, 0:1], 0) + column_to_row(curvature, cases)
    out_ref[...] = jnp.broadcast_to(row[None], (copies, 1, 128))


def final_kernel(sums_ref, direction_ref, solution_ref, out_ref, alpha_ref):
    cases, slabs, width = direction_ref.shape[:3]
    row = jnp.sum(sums_ref[...], axis=0)
    norm = row_to_column(row, 0, cases)
    curvature = row_to_column(row, cases, cases)
    alpha_ref[...] = jnp.broadcast_to(norm / curvature, (cases, 128))

    def step(case, carry):
        alpha = jnp.broadcast_to(alpha_ref[pl.ds(case, 1), :], (width, 128))
        for a in range(slabs):
            out_ref[case, a] = solution_ref[case, a] + alpha * direction_ref[case, a]
        return carry

    lax.fori_loop(0, cases, step, 0, unroll=2)


def shards(
    right_side,
    block_weight,
    across_weight,
    along_weight,
    block_stiffness,
    across_matrix,
    along_matrix,
    boundary_blocks,
    block_rows,
    block_columns,
    live_pairs,
    surface_index,
    interface_slot,
):
    cases, slabs, width, lanes = right_side.shape
    field = right_side.shape
    rows_local = block_rows[0, 0]
    columns_local = block_columns[0, 0]
    blocks_local = boundary_blocks[0, 0]
    live_local = live_pairs[0, 0]
    surface_local = surface_index[0, 0]
    half = lax.axis_index("sec").astype(jnp.int32)
    place = lax.axis_index(BLK).astype(jnp.int32)
    blk_count = lax.axis_size(BLK)
    clu_count = lax.axis_size(CLU)
    owners = 2 * blk_count
    all_count = owners * clu_count
    slot_count = interface_slot.shape[0]
    surface = surface_local.reshape(1, lanes)

    def edges_by(make):
        return edge_outputs(cases, slabs, width, lanes, make)

    def sent(edges):
        before = passed_along(edges[0], SEC_CLU, 1)
        after = passed_along(edges[1], SEC_CLU, -1)
        left = passed_along(edges[2], BLK, 1)
        right = passed_along(edges[3], BLK, -1)
        return before, after, left, right

    first_edges = [
        kept((cases + 1, width, lanes)),
        kept((cases, width, lanes)),
        kept((cases + 1, slabs, lanes)),
        kept((cases, slabs, lanes)),
    ]
    ends = jnp.stack([across_weight[-1, :], along_weight[:, -1]])
    ends = jnp.broadcast_to(ends[:, :, None], (2, width, lanes))
    trace, *edges = kernel(
        first_trace_kernel,
        (kept((blk_count, cases, lanes)), *first_edges),
        (right_side, surface, ends),
    )
    mine = exchanged(trace, BLK)
    other = partner(mine)

    owner = (interface_slot // lanes) ^ (half * blk_count)
    slot_blocks = owner.reshape(slot_count // lanes, lanes)
    slot_lanes = (interface_slot % lanes).reshape(slot_count // lanes, lanes)
    number = jnp.arange(slot_count, dtype=jnp.int32)
    lane_number = jnp.arange(lanes, dtype=jnp.int32)
    by_owner = (jnp.arange(owners, dtype=jnp.int32)[:, None] == owner[None, :]).astype(BF16)
    by_lane = (interface_slot % lanes)[:, None] == lane_number[None, :]
    parts = jnp.concatenate(
        [
            jnp.where(by_lane, (number // lanes)[:, None], 0),
            jnp.where(by_lane, (number % lanes)[:, None], 0),
        ],
        axis=1,
    ).astype(BF16)
    found = jnp.dot(by_owner, parts, preferred_element_type=F32).astype(jnp.int32)
    dof_blocks, dof_lanes = found[:, :lanes], found[:, lanes:]
    by_block = (
        jnp.arange(slabs * width, dtype=jnp.int32)[:, None] == (surface_local // lanes)[None, :]
    ).astype(BF16)
    marks = jnp.where(
        (surface_local % lanes)[:, None] == lane_number[None, :],
        jnp.arange(1, surface_local.shape[0] + 1, dtype=jnp.int32)[:, None],
        0,
    ).astype(BF16)
    inverse = (
        jnp.dot(by_block, marks, preferred_element_type=F32)
        .astype(jnp.int32)
        .reshape(slabs, width, lanes)
    )

    matrices = jnp.stack(
        [block_stiffness, across_matrix, across_matrix.T, along_matrix, along_matrix.T]
    )

    half_columns = clu_count
    slots_shape = (owners, cases, lanes)
    pairs = jnp.stack(
        [
            rows_local,
            columns_local ^ (half * half_columns),
            jnp.broadcast_to(live_local, rows_local.shape),
            jnp.broadcast_to(place, rows_local.shape),
        ]
    )
    forward_inputs = (pairs, slot_lanes, slot_blocks, near(blocks_local))

    def weights_of(halo):
        across_edge = halo[0][cases, :, 0][None, :]
        along_edge = halo[2][cases, :, 0][:, None]
        across_lower = jnp.concatenate([across_edge, across_weight[:-1, :]], axis=0)
        along_lower = jnp.concatenate([along_edge, along_weight[:, :-1]], axis=1)
        tile = jnp.arange(width, dtype=jnp.int32)[None, :]
        weights = jnp.stack(
            [
                block_weight,
                across_weight,
                across_lower,
                jnp.where(tile < width - 1, along_weight, 0.0),
                jnp.where(tile > 0, along_lower, 0.0),
                jnp.where(tile == width - 1, along_weight, 0.0),
                jnp.where(tile == 0, along_lower, 0.0),
            ]
        )
        return jnp.broadcast_to(weights[..., None], (*weights.shape, lanes))

    edge_kept, edge_like = edges_by(kept), edges_by(like)
    own_slots_shape = steps_shape = like((2, cases, lanes))
    image_outputs = (like(field), like((cases, lanes)), like((cases, lanes)), *edge_like)
    stiffness_scratch = [pltpu.VMEM((cases, slabs, lanes), F32)] * 2
    stiffness_scratch += [pltpu.VMEM((4, cases, lanes), F32)]
    solution = None
    residual = right_side
    direction = right_side
    slot_residual = slot_direction = sums = None
    for iteration in range(ITERS):
        first = iteration == 0
        last = iteration + 1 == ITERS
        deep = 2 * cases if last else cases
        scratch = [
            pltpu.VMEM((slot_count // lanes, deep, lanes), BF16),
            pltpu.VMEM((2 * half_columns, deep, lanes), F32),
        ]
        halves = (kept((half_columns, deep, lanes)),) * 2
        if not first:
            inputs = (*forward_inputs, slot_residual, slot_direction)
            inputs += (near(mine), near(other), near(sums))
            if last:
                steps, keep, send = kernel(
                    functools.partial(forward_kernel, False, True),
                    (steps_shape, *halves),
                    inputs,
                    [pltpu.VMEM(slots_shape, F32)] + scratch,
                    1,
                )
            else:
                steps, slot_residual, slot_direction, own_slots, keep, send = kernel(
                    functools.partial(forward_kernel, False, False),
                    (steps_shape, *(like(slots_shape),) * 2, own_slots_shape, *halves),
                    inputs,
                    scratch,
                    1,
                )
        if first:
            slot_direction, own_slots, keep, send = kernel(
                functools.partial(forward_kernel, True, False),
                (like(slots_shape), own_slots_shape, *halves),
                (*forward_inputs, near(mine), near(other)),
                scratch,
                1,
            )
            slot_residual = slot_direction
        pieces = keep + partner(send)
        column_pieces = exchanged(pieces, CLU)

        if first:
            halo_residual = halo_direction = sent(edges)
            given = (weights_of(halo_direction), matrices, surface)
            image, dots, image_trace, *edges = kernel(
                functools.partial(stiffness_kernel, True),
                image_outputs,
                (right_side, *halo_direction, *given),
                stiffness_scratch,
            )
        else:
            inputs = (steps, own, inverse, image, residual, direction)
            if iteration > 1:
                inputs += (solution,)
            inputs += (*halo_image, *halo_residual, *halo_direction)
            if last:
                solution, direction, dots = kernel(
                    functools.partial(field_kernel, iteration == 1, True),
                    (like(field), like(field), like((cases, lanes))),
                    (*inputs, *given),
                    [pltpu.VMEM(field, F32)] * 2
                    + [pltpu.VMEM(edge.shape, F32) for edge in halo_image]
                    + stiffness_scratch,
                )
            else:
                outs = kernel(
                    functools.partial(field_kernel, iteration == 1, False),
                    (like(field),) * 3 + edge_like * 2,
                    inputs,
                )
                solution, direction, residual = outs[:3]
                halo_residual, halo_direction = outs[3:7], outs[7:11]
            if not last:
                image, dots, image_trace, *edges = kernel(
                    functools.partial(stiffness_kernel, False),
                    image_outputs,
                    (direction, residual, *halo_direction, *given),
                    stiffness_scratch,
                )
        if last:
            rows = kernel(
                last_sums_kernel, kept((all_count, 1, lanes)), (near(column_pieces), dots)
            )
            totals = exchanged(rows, ALL)
            return kernel(
                final_kernel,
                like(field),
                (near(totals), direction, solution),
                [pltpu.VMEM((cases, lanes), F32)],
            )

        z_low = kernel(low_kernel, kept((clu_count, cases, lanes), BF16), (near(column_pieces),))
        low_mine = exchanged(z_low, CLU)
        low_other = partner(low_mine)
        keep, send = kernel(
            backward_kernel,
            (kept((blk_count, cases, lanes)),) * 2,
            (
                pairs,
                dof_lanes,
                dof_blocks,
                near(blocks_local),
                near(low_mine),
                near(low_other),
            ),
            [
                pltpu.VMEM((2 * half_columns, cases, lanes), BF16),
                pltpu.VMEM((slot_count // lanes, cases, lanes), F32),
            ],
            1,
        )
        row_pieces = keep + partner(send)
        arrived = exchanged(row_pieces, BLK)
        payload, own = kernel(
            own_kernel,
            (kept((blk_count, cases + 8, lanes)), like((cases, lanes))),
            (near(arrived), image_trace, dots, own_slots),
        )
        mine = exchanged(payload, BLK)
        edges = kernel(edges_kernel, edge_kept, (own, inverse, *edges))
        halo_image = sent(edges)
        other = partner(mine)
        row = kernel(
            functools.partial(range_sum_kernel, cases),
            kept((clu_count, 1, lanes)),
            (near(mine), near(other)),
        )
        sums = exchanged(row, CLU)


def solution(mesh):
    finer = Mesh(
        mesh.devices.reshape(mesh.shape["sec"], 4, 2, 2, 8),
        ("sec", "clu_0", "clu_1", "blk_0", "blk_1"),
    )
    placed = (
        P(None, SEC_CLU, BLK, None),
        P(SEC_CLU, BLK),
        P(SEC_CLU, BLK),
        P(SEC_CLU, BLK),
        P(),
        P(),
        P(),
        P("sec", CLU, BLK, None, None),
        P("sec", CLU, BLK),
        P("sec", CLU, BLK),
        P("sec", CLU, BLK),
        P("sec", CLU, BLK),
        P(CLU),
    )
    return jax.shard_map(
        shards, mesh=finer, in_specs=placed, out_specs=P(None, SEC_CLU, BLK, None), check_vma=False
    )
```

```python
import functools

import jax
import jax.numpy as jnp
from jax import lax
from jax.experimental import pallas as pl
from jax.experimental.pallas import tpu as pltpu
from jax.sharding import Mesh
from jax.sharding import PartitionSpec as P

ITERS = 3
ALL = ("sec", "clu_0", "clu_1", "blk_0", "blk_1")
SEC_CLU = ("sec", "clu_0", "clu_1")
BLK = ("blk_0", "blk_1")
CLU = ("clu_0", "clu_1")
F32 = jnp.float32
BF16 = jnp.bfloat16
SMEM = pl.BlockSpec(memory_space=pltpu.SMEM)
VMEM = pl.BlockSpec(memory_space=pltpu.VMEM)
LIMIT = 24 * 1024 * 1024


def passed_along(value, axis, by):
    count = lax.axis_size(axis)
    pairs = [(i, i + by) for i in range(count) if 0 <= i + by < count]
    return lax.ppermute(value, axis, pairs)


def partner(value):
    return lax.ppermute(value, "sec", [(0, 1), (1, 0)])


def exchanged(pieces, axes):
    return lax.all_to_all(pieces, axes, split_axis=0, concat_axis=0, tiled=True)


class near:
    def __init__(self, value):
        self.value = value


def kernel(body, outs, inputs, scratch=(), scalars=0):
    inputs = [
        pltpu.with_memory_space_constraint(x.value, pltpu.VMEM)
        if isinstance(x, near)
        else x
        if i < scalars
        else pltpu.with_memory_space_constraint(x, pltpu.HBM)
        for i, x in enumerate(inputs)
    ]
    return pl.pallas_call(
        body,
        out_shape=outs,
        in_specs=[SMEM] * scalars + [pl.BlockSpec()] * (len(inputs) - scalars),
        scratch_shapes=list(scratch),
        compiler_params=pltpu.CompilerParams(vmem_limit_bytes=LIMIT),
    )(*inputs)


def lanes_taken(rows, index):
    return jnp.take_along_axis(rows, index, axis=1)


def like(shape, dtype=F32):
    return pltpu.HBM(shape, dtype)


def kept(shape, dtype=F32):
    return pltpu.VMEM(shape, dtype)


def lane_iota(shape):
    return lax.broadcasted_iota(jnp.int32, shape, len(shape) - 1)


def row_iota(shape):
    return lax.broadcasted_iota(jnp.int32, shape, len(shape) - 2)


def column_to_row(column, at):
    cases = column.shape[0]
    shape = (cases, 128)
    here = lane_iota(shape) == row_iota(shape) + at
    return jnp.sum(jnp.where(here, column, 0.0), axis=0, keepdims=True)


def row_to_column(row, at, cases):
    shape = (cases, 128)
    here = lane_iota(shape) == row_iota(shape) + at
    return jnp.sum(jnp.where(here, row, 0.0), axis=1, keepdims=True)


def trace_of(ref, case, lane_index, block_index):
    slabs, width = ref.shape[1], ref.shape[2]
    sub = row_iota((width, 128))
    total = jnp.zeros((width, 128), F32)
    for a in range(slabs):
        picked = lanes_taken(ref[case, a], lane_index)
        total = jnp.where(block_index == a * width + sub, picked, total)
    return jnp.sum(total, axis=0, keepdims=True)


def edges_stored(case, a, value, slabs, edge_refs):
    before_ref, after_ref, left_ref, right_ref = edge_refs
    if a == slabs - 1:
        before_ref[case] = value
    if a == 0:
        after_ref[case] = value
    left_ref[case, a : a + 1, :] = value[-1:, :]
    right_ref[case, a : a + 1, :] = value[:1, :]


def edge_outputs(cases, slabs, width, lanes, make):
    return (make((cases, width, lanes)),) * 2 + (make((cases, slabs, lanes)),) * 2


def first_trace_kernel(field_ref, surface_ref, across_ref, along_ref, out_ref, *edge_refs):
    cases, slabs = field_ref.shape[:2]
    copies = out_ref.shape[0]
    square = across_ref.shape
    here = lax.broadcasted_iota(jnp.int32, square, 0) == lax.broadcasted_iota(jnp.int32, square, 1)
    last_row = jnp.sum(jnp.where(here, across_ref[slabs - 1 :, :], 0.0), axis=1, keepdims=True)
    edge_refs[0][cases] = jnp.broadcast_to(last_row, (square[1], 128))
    edge_refs[2][cases] = jnp.broadcast_to(along_ref[:, square[1] - 1 :], (square[0], 128))
    local = jnp.broadcast_to(surface_ref[...], (8, 128))
    lane_index, block_index = local & 127, local >> 7

    def step(case, carry):
        row = trace_of(field_ref, case, lane_index, block_index)
        out_ref[0, pl.ds(case, 1), :] = row
        for a in range(slabs):
            edges_stored(case, a, field_ref[case, a], slabs, edge_refs)
        return carry

    lax.fori_loop(0, field_ref.shape[0], step, 0, unroll=4)
    value = out_ref[0]
    for i in range(1, copies):
        out_ref[i] = value


def permuted_block(source_ref, lanes_ref, blocks_ref, d):
    count, cases = source_ref.shape[0], source_ref.shape[1]
    lane_index = jnp.broadcast_to(lanes_ref[pl.ds(d, 1), :], (8, 128))
    block_index = jnp.broadcast_to(blocks_ref[pl.ds(d, 1), :], (8, 128))
    groups = cases // 8
    totals = [jnp.zeros((8, 128), F32) for _ in range(groups)]
    for b in range(count):
        here = block_index == b
        for g in range(groups):
            picked = lanes_taken(source_ref[b, 8 * g : 8 * g + 8, :], lane_index)
            totals[g] = jnp.where(here, picked, totals[g])
    return totals


def selected_block(flat_ref, lanes_ref, blocks_ref, d, cases):
    width = flat_ref.shape[1] // 128
    wanted = jnp.broadcast_to(lanes_ref[pl.ds(d, 1), :], (128, 128))
    chosen = jnp.where(row_iota((128, 128)) == wanted, 1.0, 0.0).astype(BF16)
    chosen = jnp.concatenate([chosen] * width, axis=0)
    block_index = jnp.broadcast_to(blocks_ref[pl.ds(d, 1), :], (cases, 128))
    step = 256 // cases
    total = jnp.zeros((cases, 128), F32)
    for g in range(flat_ref.shape[0] // 256):
        found = jnp.dot(
            flat_ref[256 * g : 256 * g + 256, :], chosen, preferred_element_type=F32
        ).reshape(step, cases, 128)
        for j in range(step):
            total = jnp.where(block_index == g * step + j, found[j], total)
    return total


def high_and_low(value):
    high = value.astype(BF16)
    return high, (value - high.astype(F32)).astype(BF16)


def alpha_beta(sums_ref, cases):
    row = jnp.sum(sums_ref[...], axis=0)
    norm, curvature, crossed, squared = (row_to_column(row, i * cases, cases) for i in range(4))
    alpha = norm / curvature
    following = norm - 2.0 * alpha * crossed + alpha * alpha * squared
    beta = jnp.maximum(following, 0.0) / norm
    return alpha, beta


def forward_kernel(first, last, *refs):
    refs = list(refs)
    pairs_ref, lanes_ref, blocks_ref, *boundary_refs = refs[:5]
    refs = refs[5:]
    if first:
        mine_ref, other_ref, direction_ref, slots_ref, out_ref, low_ref, flat_ref = refs
        count = mine_ref.shape[0]
        direction_ref[:count] = mine_ref[...]
        direction_ref[count:] = other_ref[...]
    else:
        old_residual_ref, old_direction_ref, mine_ref, other_ref, sums_ref = refs[:5]
        steps_ref, refs = refs[5], refs[6:]
        if last:
            out_ref, direction_ref, low_ref, flat_ref = refs
        else:
            residual_ref, direction_ref, slots_ref, out_ref, low_ref, flat_ref = refs
        cases = old_direction_ref.shape[1]
        count = mine_ref.shape[0]
        alpha, beta = alpha_beta(sums_ref, cases)
        alpha = jnp.broadcast_to(alpha, (cases, 128))
        beta = jnp.broadcast_to(beta, (cases, 128))
        steps_ref[0] = alpha
        steps_ref[1] = beta
        for half, image_ref in ((0, mine_ref), (1, other_ref)):
            for i in range(count):
                b = half * count + i
                residual = old_residual_ref[b] - alpha * image_ref[i, :cases, :]
                if not last:
                    residual_ref[b] = residual
                direction_ref[b] = residual + beta * old_direction_ref[b]
    cases = direction_ref.shape[1]
    if not last:
        place = pairs_ref[5, 0]
        slots_ref[0] = direction_ref[place] if first else residual_ref[place]
        slots_ref[1] = direction_ref[place]

    owners = direction_ref.shape[0]
    half = owners // 2
    for i in range(0, owners, 8):
        value = direction_ref[i : i + 8].reshape(8 * cases, 128)
        if last:
            high, low = high_and_low(value)
            flat_ref[i * cases : (i + 8) * cases, :128] = high
            flat_ref[i * cases : (i + 8) * cases, 128:] = low
        else:
            flat_ref[i * cases : (i + 8) * cases, :] = value.astype(BF16)

    def step(d, carry):
        one = permuted_block(direction_ref, lanes_ref, blocks_ref, d)
        two = selected_block(flat_ref, lanes_ref, blocks_ref, half + d, cases)
        for at, value in ((d, jnp.concatenate(one, axis=0)), (half + d, two)):
            if last:
                low_ref[at] = jnp.concatenate(high_and_low(value), axis=0)
            else:
                low_ref[at] = value.astype(BF16)
        return carry

    lax.fori_loop(0, half, step, 0, unroll=2)
    out_ref[...] = jnp.zeros(out_ref.shape, F32)
    for p, block in pair_blocks(boundary_refs):
        product = jnp.dot(low_ref[pairs_ref[0, p]], block, preferred_element_type=F32)
        out_ref[pairs_ref[1, p]] += jnp.where(pairs_ref[3, p] > 0, product, 0.0)


def pair_blocks(refs):
    count = refs[0].shape[0]
    for i, ref in enumerate(refs):
        for p in range(count):
            yield i * count + p, ref[p]


def backward_kernel(
    pairs_ref,
    lanes_ref,
    blocks_ref,
    boundary_ref,
    boundary_other_ref,
    mine_ref,
    other_ref,
    out_ref,
    low_ref,
    rows_scratch,
):
    half_count = mine_ref.shape[0]
    low_ref[:half_count] = mine_ref[...]
    low_ref[half_count:] = other_ref[...]
    rows_scratch[...] = jnp.zeros(rows_scratch.shape, F32)
    for p, block in pair_blocks((boundary_ref, boundary_other_ref)):
        product = lax.dot_general(
            low_ref[pairs_ref[2, p]],
            block,
            (((1,), (1,)), ((), ())),
            preferred_element_type=F32,
        )
        rows_scratch[pairs_ref[0, p]] += jnp.where(pairs_ref[4, p] > 0, product, 0.0)

    def step(d, carry):
        for g, total in enumerate(permuted_block(rows_scratch, lanes_ref, blocks_ref, d)):
            out_ref[d, 8 * g : 8 * g + 8, :] = total
        return carry

    lax.fori_loop(0, out_ref.shape[0], step, 0, unroll=4)


def low_kernel(pieces_ref, out_ref):
    low = jnp.sum(pieces_ref[...], axis=0).astype(BF16)
    for i in range(out_ref.shape[0]):
        out_ref[i] = low


def stiffness(direction_ref, residual_ref, halo_refs, given_refs, out_refs, scratch_refs):
    before_ref, after_ref, left_ref, right_ref = halo_refs
    weights_ref, matrices_ref, surface_ref = given_refs
    image_ref, dots_ref, *more_refs = out_refs
    low_ref, high_ref, sums_ref = scratch_refs
    want_trace = len(more_refs) > 0
    cases, slabs, width = direction_ref.shape[:3]
    rows = cases * width

    def product(value, which):
        return jnp.dot(
            value.reshape(rows, 128).astype(BF16),
            matrices_ref[which],
            preferred_element_type=F32,
        ).reshape(cases, width, 128)

    def taken(a):
        if a < 0:
            return before_ref[:cases]
        if a == slabs:
            return after_ref[...]
        return direction_ref[:, a]

    high_ref[...] = product(right_ref[...], 3)
    low_ref[...] = product(left_ref[:cases], 4)
    for a in range(slabs):
        own = taken(a)
        result = weights_ref[0, a][None] * product(own, 0)
        result = result - weights_ref[1, a][None] * product(taken(a + 1), 1)
        result = result - weights_ref[2, a][None] * product(taken(a - 1), 2)
        result = result - weights_ref[3, a][None] * pltpu.roll(product(own, 3), width - 1, 1)
        result = result - weights_ref[4, a][None] * pltpu.roll(product(own, 4), 1, 1)
        result = result - weights_ref[5, a][None] * high_ref[:, a : a + 1, :]
        result = result - weights_ref[6, a][None] * low_ref[:, a : a + 1, :]
        image_ref[:, a] = result
    local = jnp.broadcast_to(surface_ref[...], (8, 128))
    lane_index, block_index = local & 127, local >> 7

    def step(case, carry):
        r = residual_ref[case]
        d = direction_ref[case]
        q = image_ref[case]
        pairs = ((r, r), (d, q), (r, q), (q, q)) if want_trace else ((r, r), (d, q))
        for i, (one, two) in enumerate(pairs):
            sums_ref[i, pl.ds(case, 1), :] = jnp.sum(
                jnp.sum(one * two, axis=0), axis=0, keepdims=True
            )
        if want_trace:
            more_refs[0][pl.ds(case, 1), :] = trace_of(image_ref, case, lane_index, block_index)
            for a in range(slabs):
                edges_stored(case, a, image_ref[case, a], slabs, more_refs[1:])
        return carry

    lax.fori_loop(0, cases, step, 0, unroll=4)
    lane = lane_iota((cases, 128))
    dots = jnp.zeros((cases, 128), F32)
    for i in range(4 if want_trace else 2):
        dots = jnp.where(lane == i, jnp.sum(sums_ref[i], axis=1, keepdims=True), dots)
    dots_ref[...] = dots


def stiffness_kernel(same, direction_ref, *refs):
    residual_ref, refs = (direction_ref, refs) if same else (refs[0], refs[1:])
    stiffness(direction_ref, residual_ref, refs[:4], refs[4:7], refs[7:14], refs[14:])


def field_kernel(first, last, *refs):
    refs = list(refs)

    def take(n):
        taken = refs[:n]
        del refs[:n]
        return taken

    steps_ref, own_ref, inverse_ref, image_ref, residual_ref, direction_ref = take(6)
    solution_ref = None if first else take(1)[0]
    halo_image_refs, halo_residual_refs, halo_direction_refs = take(4), take(4), take(4)
    given_refs = take(3) if last else None
    new_solution_ref, new_direction_ref = take(2)
    if last:
        (dots_ref,) = take(1)
        new_residual_ref, new_image_ref = take(2)
        new_halo_direction_refs = take(4)
        new_halo_residual_refs = None
        out_refs = (new_image_ref, dots_ref)
    else:
        (new_residual_ref,) = take(1)
        new_halo_residual_refs, new_halo_direction_refs = take(4), take(4)
    cases, slabs, width = direction_ref.shape[:3]

    def step(case, carry):
        alpha = jnp.broadcast_to(steps_ref[0, pl.ds(case, 1), :], (width, 128))
        beta = jnp.broadcast_to(steps_ref[1, pl.ds(case, 1), :], (width, 128))
        own = jnp.broadcast_to(own_ref[pl.ds(case, 1), :], (width, 128))
        for i in range(4):
            r = halo_residual_refs[i][case] - alpha * halo_image_refs[i][case]
            if not last:
                new_halo_residual_refs[i][case] = r
            new_halo_direction_refs[i][case] = r + beta * halo_direction_refs[i][case]
        for a in range(slabs):
            slot = inverse_ref[a]
            there = slot > 0
            extra = lanes_taken(own, jnp.where(there, slot - 1, 0))
            image = image_ref[case, a] + jnp.where(there, extra, 0.0)
            d = direction_ref[case, a]
            r = residual_ref[case, a] - alpha * image
            new_residual_ref[case, a] = r
            moved = alpha * d
            if solution_ref is not None:
                moved = solution_ref[case, a] + moved
            new_solution_ref[case, a] = moved
            new_direction_ref[case, a] = r + beta * d
        return carry

    lax.fori_loop(0, cases, step, 0, unroll=4)
    if last:
        halo_refs = new_halo_direction_refs
        stiffness(new_direction_ref, new_residual_ref, halo_refs, given_refs, out_refs, refs)


def own_kernel(arrived_ref, trace_ref, dots_ref, slots_ref, out_ref, own_ref):
    copies, cases = out_ref.shape[0], trace_ref.shape[0]
    y = jnp.sum(arrived_ref[...], axis=0)
    own_ref[...] = y
    trace = trace_ref[...]
    r = slots_ref[0]
    d = slots_ref[1]
    dots = dots_ref[...]
    terms = (None, d * y, r * y, (2.0 * trace + y) * y)
    row = jnp.zeros((1, 128), F32)
    for i, term in enumerate(terms):
        column = dots[:, i : i + 1]
        if term is not None:
            column = column + jnp.sum(term, axis=1, keepdims=True)
        row = row + column_to_row(column, i * cases)
    image = trace + y
    rows = jnp.broadcast_to(row, (8, 128))
    for i in range(copies):
        out_ref[i, :cases, :] = image
        out_ref[i, cases:, :] = rows


def range_sum_kernel(cases, mine_ref, other_ref, out_ref):
    row = jnp.sum(mine_ref[:, cases:, :], axis=0) + jnp.sum(other_ref[:, cases:, :], axis=0)
    out_ref[...] = jnp.broadcast_to(row[0:1, :][None], out_ref.shape)


def edges_kernel(own_ref, inverse_ref, *refs):
    edge_refs, new_edge_refs = refs[:4], refs[4:]
    slabs, width = inverse_ref.shape[:2]
    sides = (
        inverse_ref[slabs - 1],
        inverse_ref[0],
        jnp.concatenate([inverse_ref[a, width - 1 :, :] for a in range(slabs)], axis=0),
        jnp.concatenate([inverse_ref[a, :1, :] for a in range(slabs)], axis=0),
    )

    def step(case, carry):
        values = jnp.broadcast_to(own_ref[pl.ds(case, 1), :], (8, 128))
        for slot, edge_ref, new_edge_ref in zip(sides, edge_refs, new_edge_refs):
            there = slot > 0
            extra = lanes_taken(values, jnp.where(there, slot - 1, 0))
            new_edge_ref[case] = edge_ref[case] + jnp.where(there, extra, 0.0)
        return carry

    lax.fori_loop(0, own_ref.shape[0], step, 0, unroll=4)


def last_sums_kernel(arrived_ref, dots_ref, out_ref):
    copies = out_ref.shape[0]
    cases = dots_ref.shape[0]
    total = jnp.sum(arrived_ref[...], axis=0)
    z = total[:cases]
    rest = total[cases:]
    low = z.astype(BF16).astype(F32)
    dots = dots_ref[...]
    curvature = dots[:, 1:2] + jnp.sum((z + rest) * low, axis=1, keepdims=True)
    row = column_to_row(dots[:, 0:1], 0) + column_to_row(curvature, cases)
    out_ref[...] = jnp.broadcast_to(row[None], (copies, 1, 128))


def final_kernel(sums_ref, direction_ref, solution_ref, out_ref, alpha_ref):
    cases, slabs, width = direction_ref.shape[:3]
    row = jnp.sum(sums_ref[...], axis=0)
    norm = row_to_column(row, 0, cases)
    curvature = row_to_column(row, cases, cases)
    alpha_ref[...] = jnp.broadcast_to(norm / curvature, (cases, 128))

    def step(case, carry):
        alpha = jnp.broadcast_to(alpha_ref[pl.ds(case, 1), :], (width, 128))
        for a in range(slabs):
            out_ref[case, a] = solution_ref[case, a] + alpha * direction_ref[case, a]
        return carry

    lax.fori_loop(0, cases, step, 0, unroll=2)


def shards(
    right_side,
    block_weight,
    across_weight,
    along_weight,
    block_stiffness,
    across_matrix,
    along_matrix,
    boundary_blocks,
    block_rows,
    block_columns,
    live_pairs,
    surface_index,
    interface_slot,
):
    cases, slabs, width, lanes = right_side.shape
    field = right_side.shape
    rows_local = block_rows[0, 0]
    columns_local = block_columns[0, 0]
    blocks_local = boundary_blocks[0, 0]
    live_local = live_pairs[0, 0]
    surface_local = surface_index[0, 0]
    half = lax.axis_index("sec").astype(jnp.int32)
    place = lax.axis_index(BLK).astype(jnp.int32)
    blk_count = lax.axis_size(BLK)
    clu_count = lax.axis_size(CLU)
    owners = 2 * blk_count
    all_count = owners * clu_count
    slot_count = interface_slot.shape[0]
    surface = surface_local.reshape(1, lanes)

    def edges_by(make):
        return edge_outputs(cases, slabs, width, lanes, make)

    def sent(edges):
        before = passed_along(edges[0], SEC_CLU, 1)
        after = passed_along(edges[1], SEC_CLU, -1)
        left = passed_along(edges[2], BLK, 1)
        right = passed_along(edges[3], BLK, -1)
        return before, after, left, right

    first_edges = [
        kept((cases + 1, width, lanes)),
        kept((cases, width, lanes)),
        kept((cases + 1, slabs, lanes)),
        kept((cases, slabs, lanes)),
    ]
    trace, *edges = kernel(
        first_trace_kernel,
        (like((blk_count, cases, lanes)), *first_edges),
        (right_side, surface, across_weight, along_weight),
    )
    mine = exchanged(trace, BLK)
    other = partner(mine)

    owner = (interface_slot // lanes) ^ (half * blk_count)
    slot_blocks = owner.reshape(slot_count // lanes, lanes)
    slot_lanes = (interface_slot % lanes).reshape(slot_count // lanes, lanes)
    number = jnp.arange(slot_count, dtype=jnp.int32)
    lane_number = jnp.arange(lanes, dtype=jnp.int32)
    by_owner = (jnp.arange(owners, dtype=jnp.int32)[:, None] == owner[None, :]).astype(BF16)
    by_lane = (interface_slot % lanes)[:, None] == lane_number[None, :]
    parts = jnp.concatenate(
        [
            jnp.where(by_lane, (number // lanes)[:, None], 0),
            jnp.where(by_lane, (number % lanes)[:, None], 0),
        ],
        axis=1,
    ).astype(BF16)
    found = jnp.dot(by_owner, parts, preferred_element_type=F32).astype(jnp.int32)
    dof_blocks, dof_lanes = found[:, :lanes], found[:, lanes:]
    by_block = (
        jnp.arange(slabs * width, dtype=jnp.int32)[:, None] == (surface_local // lanes)[None, :]
    ).astype(BF16)
    marks = jnp.where(
        (surface_local % lanes)[:, None] == lane_number[None, :],
        jnp.arange(1, surface_local.shape[0] + 1, dtype=jnp.int32)[:, None],
        0,
    ).astype(BF16)
    inverse = (
        jnp.dot(by_block, marks, preferred_element_type=F32)
        .astype(jnp.int32)
        .reshape(slabs, width, lanes)
    )

    matrices = jnp.stack(
        [block_stiffness, across_matrix, across_matrix.T, along_matrix, along_matrix.T]
    )

    half_columns = clu_count
    slots_shape = (owners, cases, lanes)
    live = jnp.arange(rows_local.shape[0], dtype=jnp.int32) < live_local
    listed = jnp.stack([rows_local, columns_local, live.astype(jnp.int32)])
    blocks_other = partner(blocks_local)
    listed_other = partner(listed)
    listed = jnp.concatenate([listed, listed_other], axis=1)
    in_half = listed[1] // half_columns == half
    pairs = jnp.stack(
        [
            listed[0],
            listed[1] % half_columns,
            listed[1] ^ (half * half_columns),
            jnp.where(in_half, listed[2], 0),
            listed[2],
            jnp.broadcast_to(place, listed[0].shape),
        ]
    )
    forward_inputs = (pairs, slot_lanes, slot_blocks, near(blocks_local), near(blocks_other))

    def weights_of(halo):
        across_edge = halo[0][cases, :, 0][None, :]
        along_edge = halo[2][cases, :, 0][:, None]
        across_lower = jnp.concatenate([across_edge, across_weight[:-1, :]], axis=0)
        along_lower = jnp.concatenate([along_edge, along_weight[:, :-1]], axis=1)
        tile = jnp.arange(width, dtype=jnp.int32)[None, :]
        weights = jnp.stack(
            [
                block_weight,
                across_weight,
                across_lower,
                jnp.where(tile < width - 1, along_weight, 0.0),
                jnp.where(tile > 0, along_lower, 0.0),
                jnp.where(tile == width - 1, along_weight, 0.0),
                jnp.where(tile == 0, along_lower, 0.0),
            ]
        )
        return jnp.broadcast_to(weights[..., None], (*weights.shape, lanes))

    edge_kept, edge_like = edges_by(kept), edges_by(like)
    own_slots_shape = steps_shape = like((2, cases, lanes))
    image_outputs = (like(field), like((cases, lanes)), like((cases, lanes)), *edge_like)
    stiffness_scratch = [pltpu.VMEM((cases, slabs, lanes), F32)] * 2
    stiffness_scratch += [pltpu.VMEM((4, cases, lanes), F32)]
    solution = None
    residual = right_side
    direction = right_side
    slot_residual = slot_direction = sums = None
    for iteration in range(ITERS):
        first = iteration == 0
        last = iteration + 1 == ITERS
        deep = 2 * cases if last else cases
        scratch = [
            pltpu.VMEM((slot_count // lanes, deep, lanes), BF16),
            pltpu.VMEM((owners * cases, 2 * lanes if last else lanes), BF16),
        ]
        column_sums = like((half_columns, deep, lanes))
        if not first:
            inputs = (*forward_inputs, slot_residual, slot_direction)
            inputs += (mine, other, near(sums))
            if last:
                steps, pieces = kernel(
                    functools.partial(forward_kernel, False, True),
                    (steps_shape, column_sums),
                    inputs,
                    [pltpu.VMEM(slots_shape, F32)] + scratch,
                    1,
                )
            else:
                steps, slot_residual, slot_direction, own_slots, pieces = kernel(
                    functools.partial(forward_kernel, False, False),
                    (steps_shape, *(like(slots_shape),) * 2, own_slots_shape, column_sums),
                    inputs,
                    scratch,
                    1,
                )
        if first:
            slot_direction, own_slots, pieces = kernel(
                functools.partial(forward_kernel, True, False),
                (like(slots_shape), own_slots_shape, column_sums),
                (*forward_inputs, near(mine), near(other)),
                scratch,
                1,
            )
            slot_residual = slot_direction
        column_pieces = exchanged(pieces, CLU)

        if first:
            halo_residual = halo_direction = sent(edges)
            given = (weights_of(halo_direction), matrices, surface)
            image, dots, image_trace, *edges = kernel(
                functools.partial(stiffness_kernel, True),
                image_outputs,
                (right_side, *halo_direction, *given),
                stiffness_scratch,
            )
        else:
            inputs = (steps, own, inverse, image, residual, direction)
            if iteration > 1:
                inputs += (solution,)
            inputs += (*halo_image, *halo_residual, *halo_direction)
            if last:
                solution, direction, dots = kernel(
                    functools.partial(field_kernel, iteration == 1, True),
                    (like(field), like(field), like((cases, lanes))),
                    (*inputs, *given),
                    [pltpu.VMEM(field, F32)] * 2
                    + [pltpu.VMEM(edge.shape, F32) for edge in halo_image]
                    + stiffness_scratch,
                )
            else:
                outs = kernel(
                    functools.partial(field_kernel, iteration == 1, False),
                    (like(field),) * 3 + edge_like * 2,
                    inputs,
                )
                solution, direction, residual = outs[:3]
                halo_residual, halo_direction = outs[3:7], outs[7:11]
            if not last:
                image, dots, image_trace, *edges = kernel(
                    functools.partial(stiffness_kernel, False),
                    image_outputs,
                    (direction, residual, *halo_direction, *given),
                    stiffness_scratch,
                )
        if last:
            rows = kernel(
                last_sums_kernel, kept((all_count, 1, lanes)), (near(column_pieces), dots)
            )
            totals = exchanged(rows, ALL)
            return kernel(
                final_kernel,
                like(field),
                (near(totals), direction, solution),
                [pltpu.VMEM((cases, lanes), F32)],
            )

        z_low = kernel(low_kernel, like((clu_count, cases, lanes), BF16), (near(column_pieces),))
        low_mine = exchanged(z_low, CLU)
        low_other = partner(low_mine)
        row_pieces = kernel(
            backward_kernel,
            like((blk_count, cases, lanes)),
            (
                pairs,
                dof_lanes,
                dof_blocks,
                near(blocks_local),
                near(blocks_other),
                near(low_mine),
                near(low_other),
            ),
            [
                pltpu.VMEM((2 * half_columns, cases, lanes), BF16),
                pltpu.VMEM((slot_count // lanes, cases, lanes), F32),
            ],
            1,
        )
        arrived = exchanged(row_pieces, BLK)
        payload, own = kernel(
            own_kernel,
            (like((blk_count, cases + 8, lanes)), like((cases, lanes))),
            (near(arrived), image_trace, dots, own_slots),
        )
        mine = exchanged(payload, BLK)
        edges = kernel(edges_kernel, edge_kept, (own, inverse, *edges))
        halo_image = sent(edges)
        other = partner(mine)
        row = kernel(
            functools.partial(range_sum_kernel, cases), like((clu_count, 1, lanes)), (mine, other)
        )
        sums = exchanged(row, CLU)


def solution(mesh):
    finer = Mesh(
        mesh.devices.reshape(mesh.shape["sec"], 4, 2, 2, 8),
        ("sec", "clu_0", "clu_1", "blk_0", "blk_1"),
    )
    placed = (
        P(None, SEC_CLU, BLK, None),
        P(SEC_CLU, BLK),
        P(SEC_CLU, BLK),
        P(SEC_CLU, BLK),
        P(),
        P(),
        P(),
        P("sec", CLU, BLK, None, None),
        P("sec", CLU, BLK),
        P("sec", CLU, BLK),
        P("sec", CLU, BLK),
        P("sec", CLU, BLK),
        P(CLU),
    )
    return jax.shard_map(
        shards, mesh=finer, in_specs=placed, out_specs=P(None, SEC_CLU, BLK, None), check_vma=False
    )
```

```python
import functools

import jax
import jax.numpy as jnp
from jax import lax
from jax.experimental import pallas as pl
from jax.experimental.pallas import tpu as pltpu
from jax.sharding import Mesh
from jax.sharding import PartitionSpec as P

ITERS = 3
ALL = ("sec", "clu_0", "clu_1", "blk_0", "blk_1")
SEC_CLU = ("sec", "clu_0", "clu_1")
BLK = ("blk_0", "blk_1")
CLU = ("clu_0", "clu_1")
F32 = jnp.float32
BF16 = jnp.bfloat16
SMEM = pl.BlockSpec(memory_space=pltpu.SMEM)
VMEM = pl.BlockSpec(memory_space=pltpu.VMEM)
LIMIT = 24 * 1024 * 1024


def passed_along(value, axis, by):
    count = lax.axis_size(axis)
    pairs = [(i, i + by) for i in range(count) if 0 <= i + by < count]
    return lax.ppermute(value, axis, pairs)


def partner(value):
    return lax.ppermute(value, "sec", [(0, 1), (1, 0)])


def exchanged(pieces, axes):
    return lax.all_to_all(pieces, axes, split_axis=0, concat_axis=0, tiled=True)


class near:
    def __init__(self, value):
        self.value = value


def kernel(body, outs, inputs, scratch=(), scalars=0):
    inputs = [
        pltpu.with_memory_space_constraint(x.value, pltpu.VMEM)
        if isinstance(x, near)
        else x
        if i < scalars
        else pltpu.with_memory_space_constraint(x, pltpu.HBM)
        for i, x in enumerate(inputs)
    ]
    return pl.pallas_call(
        body,
        out_shape=outs,
        in_specs=[SMEM] * scalars + [pl.BlockSpec()] * (len(inputs) - scalars),
        scratch_shapes=list(scratch),
        compiler_params=pltpu.CompilerParams(vmem_limit_bytes=LIMIT),
    )(*inputs)


def lanes_taken(rows, index):
    return jnp.take_along_axis(rows, index, axis=1)


def like(shape, dtype=F32):
    return pltpu.HBM(shape, dtype)


def kept(shape, dtype=F32):
    return pltpu.VMEM(shape, dtype)


def lane_iota(shape):
    return lax.broadcasted_iota(jnp.int32, shape, len(shape) - 1)


def row_iota(shape):
    return lax.broadcasted_iota(jnp.int32, shape, len(shape) - 2)


def column_to_row(column, at):
    cases = column.shape[0]
    shape = (cases, 128)
    here = lane_iota(shape) == row_iota(shape) + at
    return jnp.sum(jnp.where(here, column, 0.0), axis=0, keepdims=True)


def row_to_column(row, at, cases):
    shape = (cases, 128)
    here = lane_iota(shape) == row_iota(shape) + at
    return jnp.sum(jnp.where(here, row, 0.0), axis=1, keepdims=True)


def trace_of(ref, case, lane_index, block_index):
    slabs, width = ref.shape[1], ref.shape[2]
    sub = row_iota((width, 128))
    total = jnp.zeros((width, 128), F32)
    for a in range(slabs):
        picked = lanes_taken(ref[case, a], lane_index)
        total = jnp.where(block_index == a * width + sub, picked, total)
    return jnp.sum(total, axis=0, keepdims=True)


def edges_stored(case, a, value, slabs, edge_refs):
    before_ref, after_ref, left_ref, right_ref = edge_refs
    if a == slabs - 1:
        before_ref[case] = value
    if a == 0:
        after_ref[case] = value
    left_ref[case, a : a + 1, :] = value[-1:, :]
    right_ref[case, a : a + 1, :] = value[:1, :]


def edge_outputs(cases, slabs, width, lanes, make):
    return (make((cases, width, lanes)),) * 2 + (make((cases, slabs, lanes)),) * 2


def first_trace_kernel(field_ref, surface_ref, across_ref, along_ref, out_ref, *edge_refs):
    cases, slabs = field_ref.shape[:2]
    copies = out_ref.shape[0]
    square = across_ref.shape
    here = lax.broadcasted_iota(jnp.int32, square, 0) == lax.broadcasted_iota(jnp.int32, square, 1)
    last_row = jnp.sum(jnp.where(here, across_ref[slabs - 1 :, :], 0.0), axis=1, keepdims=True)
    edge_refs[0][cases] = jnp.broadcast_to(last_row, (square[1], 128))
    edge_refs[2][cases] = jnp.broadcast_to(along_ref[:, square[1] - 1 :], (square[0], 128))
    local = jnp.broadcast_to(surface_ref[...], (8, 128))
    lane_index, block_index = local & 127, local >> 7

    def step(case, carry):
        row = trace_of(field_ref, case, lane_index, block_index)
        out_ref[0, pl.ds(case, 1), :] = row
        for a in range(slabs):
            edges_stored(case, a, field_ref[case, a], slabs, edge_refs)
        return carry

    lax.fori_loop(0, field_ref.shape[0], step, 0, unroll=4)
    value = out_ref[0]
    for i in range(1, copies):
        out_ref[i] = value


def permuted_block(source_ref, lanes_ref, blocks_ref, d):
    count, cases = source_ref.shape[0], source_ref.shape[1]
    lane_index = jnp.broadcast_to(lanes_ref[pl.ds(d, 1), :], (8, 128))
    block_index = jnp.broadcast_to(blocks_ref[pl.ds(d, 1), :], (8, 128))
    groups = cases // 8
    totals = [jnp.zeros((8, 128), F32) for _ in range(groups)]
    for b in range(count):
        here = block_index == b
        for g in range(groups):
            picked = lanes_taken(source_ref[b, 8 * g : 8 * g + 8, :], lane_index)
            totals[g] = jnp.where(here, picked, totals[g])
    return totals


def selected_block(flat_ref, lanes_ref, blocks_ref, d, cases):
    width = flat_ref.shape[1] // 128
    wanted = jnp.broadcast_to(lanes_ref[pl.ds(d, 1), :], (128, 128))
    chosen = jnp.where(row_iota((128, 128)) == wanted, 1.0, 0.0).astype(BF16)
    chosen = jnp.concatenate([chosen] * width, axis=0)
    block_index = jnp.broadcast_to(blocks_ref[pl.ds(d, 1), :], (cases, 128))
    step = 256 // cases
    total = jnp.zeros((cases, 128), F32)
    for g in range(flat_ref.shape[0] // 256):
        found = jnp.dot(
            flat_ref[256 * g : 256 * g + 256, :], chosen, preferred_element_type=F32
        ).reshape(step, cases, 128)
        for j in range(step):
            total = jnp.where(block_index == g * step + j, found[j], total)
    return total


def high_and_low(value):
    high = value.astype(BF16)
    return high, (value - high.astype(F32)).astype(BF16)


def alpha_beta(sums_ref, cases):
    row = jnp.sum(sums_ref[...], axis=0)
    norm, curvature, crossed, squared = (row_to_column(row, i * cases, cases) for i in range(4))
    alpha = norm / curvature
    following = norm - 2.0 * alpha * crossed + alpha * alpha * squared
    beta = jnp.maximum(following, 0.0) / norm
    return alpha, beta


def forward_kernel(first, last, *refs):
    refs = list(refs)
    pairs_ref, lanes_ref, blocks_ref, boundary_ref = refs[:4]
    refs = refs[4:]
    if first:
        mine_ref, other_ref, direction_ref, slots_ref, keep_ref, send_ref, low_ref = refs[:7]
        rest = refs[7:]
        count = mine_ref.shape[0]
        direction_ref[:count] = mine_ref[...]
        direction_ref[count:] = other_ref[...]
    else:
        old_residual_ref, old_direction_ref, mine_ref, other_ref, sums_ref = refs[:5]
        steps_ref, refs = refs[5], refs[6:]
        if last:
            keep_ref, send_ref, direction_ref, low_ref = refs[:4]
            rest = refs[4:]
        else:
            residual_ref, direction_ref, slots_ref, keep_ref, send_ref, low_ref = refs[:6]
            rest = refs[6:]
        cases = old_direction_ref.shape[1]
        count = mine_ref.shape[0]
        alpha, beta = alpha_beta(sums_ref, cases)
        alpha = jnp.broadcast_to(alpha, (cases, 128))
        beta = jnp.broadcast_to(beta, (cases, 128))
        steps_ref[0] = alpha
        steps_ref[1] = beta
        for half, image_ref in ((0, mine_ref), (1, other_ref)):
            for i in range(count):
                b = half * count + i
                residual = old_residual_ref[b] - alpha * image_ref[i, :cases, :]
                if not last:
                    residual_ref[b] = residual
                direction_ref[b] = residual + beta * old_direction_ref[b]
    cases = direction_ref.shape[1]
    sums_scratch, flat_ref = rest
    if not last:
        place = pairs_ref[3, 0]
        slots_ref[0] = direction_ref[place] if first else residual_ref[place]
        slots_ref[1] = direction_ref[place]

    owners = direction_ref.shape[0]
    half = owners // 2
    for i in range(0, owners, 8):
        value = direction_ref[i : i + 8].reshape(8 * cases, 128)
        if last:
            high, low = high_and_low(value)
            flat_ref[i * cases : (i + 8) * cases, :128] = high
            flat_ref[i * cases : (i + 8) * cases, 128:] = low
        else:
            flat_ref[i * cases : (i + 8) * cases, :] = value.astype(BF16)

    def step(d, carry):
        one = permuted_block(direction_ref, lanes_ref, blocks_ref, d)
        two = selected_block(flat_ref, lanes_ref, blocks_ref, half + d, cases)
        for at, value in ((d, jnp.concatenate(one, axis=0)), (half + d, two)):
            if last:
                low_ref[at] = jnp.concatenate(high_and_low(value), axis=0)
            else:
                low_ref[at] = value.astype(BF16)
        return carry

    lax.fori_loop(0, half, step, 0, unroll=2)
    half_count = keep_ref.shape[0]
    sums_scratch[...] = jnp.zeros(sums_scratch.shape, F32)
    live = pairs_ref[2, 0]
    for p in range(boundary_ref.shape[0]):
        product = jnp.dot(low_ref[pairs_ref[0, p]], boundary_ref[p], preferred_element_type=F32)
        product = jnp.where(p < live, product, 0.0)
        sums_scratch[pairs_ref[1, p]] += product
    keep_ref[...] = sums_scratch[:half_count]
    send_ref[...] = sums_scratch[half_count:]


def backward_kernel(
    pairs_ref,
    lanes_ref,
    blocks_ref,
    boundary_ref,
    mine_ref,
    other_ref,
    keep_ref,
    send_ref,
    low_ref,
    rows_scratch,
):
    half_count = mine_ref.shape[0]
    low_ref[:half_count] = mine_ref[...]
    low_ref[half_count:] = other_ref[...]
    rows_scratch[...] = jnp.zeros(rows_scratch.shape, F32)
    live = pairs_ref[2, 0]
    for p in range(boundary_ref.shape[0]):
        product = lax.dot_general(
            low_ref[pairs_ref[1, p]],
            boundary_ref[p],
            (((1,), (1,)), ((), ())),
            preferred_element_type=F32,
        )
        product = jnp.where(p < live, product, 0.0)
        rows_scratch[pairs_ref[0, p]] += product
    count = keep_ref.shape[0]
    for at, out_ref in ((0, keep_ref), (count, send_ref)):

        def step(d, carry, at=at, out_ref=out_ref):
            totals = permuted_block(rows_scratch, lanes_ref, blocks_ref, at + d)
            for g, total in enumerate(totals):
                out_ref[d, 8 * g : 8 * g + 8, :] = total
            return carry

        lax.fori_loop(0, count, step, 0, unroll=4)


def low_kernel(pieces_ref, out_ref):
    low = jnp.sum(pieces_ref[...], axis=0).astype(BF16)
    for i in range(out_ref.shape[0]):
        out_ref[i] = low


def stiffness(direction_ref, residual_ref, halo_refs, given_refs, out_refs, scratch_refs):
    before_ref, after_ref, left_ref, right_ref = halo_refs
    weights_ref, matrices_ref, surface_ref = given_refs
    image_ref, dots_ref, *more_refs = out_refs
    low_ref, high_ref, sums_ref = scratch_refs
    want_trace = len(more_refs) > 0
    cases, slabs, width = direction_ref.shape[:3]
    rows = cases * width

    def product(value, which):
        return jnp.dot(
            value.reshape(rows, 128).astype(BF16),
            matrices_ref[which],
            preferred_element_type=F32,
        ).reshape(cases, width, 128)

    def taken(a):
        if a < 0:
            return before_ref[:cases]
        if a == slabs:
            return after_ref[...]
        return direction_ref[:, a]

    high_ref[...] = product(right_ref[...], 3)
    low_ref[...] = product(left_ref[:cases], 4)
    for a in range(slabs):
        own = taken(a)
        result = weights_ref[0, a][None] * product(own, 0)
        result = result - weights_ref[1, a][None] * product(taken(a + 1), 1)
        result = result - weights_ref[2, a][None] * product(taken(a - 1), 2)
        result = result - weights_ref[3, a][None] * pltpu.roll(product(own, 3), width - 1, 1)
        result = result - weights_ref[4, a][None] * pltpu.roll(product(own, 4), 1, 1)
        result = result - weights_ref[5, a][None] * high_ref[:, a : a + 1, :]
        result = result - weights_ref[6, a][None] * low_ref[:, a : a + 1, :]
        image_ref[:, a] = result
    local = jnp.broadcast_to(surface_ref[...], (8, 128))
    lane_index, block_index = local & 127, local >> 7

    def step(case, carry):
        r = residual_ref[case]
        d = direction_ref[case]
        q = image_ref[case]
        pairs = ((r, r), (d, q), (r, q), (q, q)) if want_trace else ((r, r), (d, q))
        for i, (one, two) in enumerate(pairs):
            sums_ref[i, pl.ds(case, 1), :] = jnp.sum(
                jnp.sum(one * two, axis=0), axis=0, keepdims=True
            )
        if want_trace:
            more_refs[0][pl.ds(case, 1), :] = trace_of(image_ref, case, lane_index, block_index)
            for a in range(slabs):
                edges_stored(case, a, image_ref[case, a], slabs, more_refs[1:])
        return carry

    lax.fori_loop(0, cases, step, 0, unroll=4)
    lane = lane_iota((cases, 128))
    dots = jnp.zeros((cases, 128), F32)
    for i in range(4 if want_trace else 2):
        dots = jnp.where(lane == i, jnp.sum(sums_ref[i], axis=1, keepdims=True), dots)
    dots_ref[...] = dots


def stiffness_kernel(same, direction_ref, *refs):
    residual_ref, refs = (direction_ref, refs) if same else (refs[0], refs[1:])
    stiffness(direction_ref, residual_ref, refs[:4], refs[4:7], refs[7:14], refs[14:])


def field_kernel(first, last, *refs):
    refs = list(refs)

    def take(n):
        taken = refs[:n]
        del refs[:n]
        return taken

    steps_ref, own_ref, inverse_ref, image_ref, residual_ref, direction_ref = take(6)
    solution_ref = None if first else take(1)[0]
    halo_image_refs, halo_residual_refs, halo_direction_refs = take(4), take(4), take(4)
    given_refs = take(3) if last else None
    new_solution_ref, new_direction_ref = take(2)
    if last:
        (dots_ref,) = take(1)
        new_residual_ref, new_image_ref = take(2)
        new_halo_direction_refs = take(4)
        new_halo_residual_refs = None
        out_refs = (new_image_ref, dots_ref)
    else:
        (new_residual_ref,) = take(1)
        new_halo_residual_refs, new_halo_direction_refs = take(4), take(4)
    cases, slabs, width = direction_ref.shape[:3]

    def step(case, carry):
        alpha = jnp.broadcast_to(steps_ref[0, pl.ds(case, 1), :], (width, 128))
        beta = jnp.broadcast_to(steps_ref[1, pl.ds(case, 1), :], (width, 128))
        own = jnp.broadcast_to(own_ref[pl.ds(case, 1), :], (width, 128))
        for i in range(4):
            r = halo_residual_refs[i][case] - alpha * halo_image_refs[i][case]
            if not last:
                new_halo_residual_refs[i][case] = r
            new_halo_direction_refs[i][case] = r + beta * halo_direction_refs[i][case]
        for a in range(slabs):
            slot = inverse_ref[a]
            there = slot > 0
            extra = lanes_taken(own, jnp.where(there, slot - 1, 0))
            image = image_ref[case, a] + jnp.where(there, extra, 0.0)
            d = direction_ref[case, a]
            r = residual_ref[case, a] - alpha * image
            new_residual_ref[case, a] = r
            moved = alpha * d
            if solution_ref is not None:
                moved = solution_ref[case, a] + moved
            new_solution_ref[case, a] = moved
            new_direction_ref[case, a] = r + beta * d
        return carry

    lax.fori_loop(0, cases, step, 0, unroll=4)
    if last:
        halo_refs = new_halo_direction_refs
        stiffness(new_direction_ref, new_residual_ref, halo_refs, given_refs, out_refs, refs)


def own_kernel(arrived_ref, trace_ref, dots_ref, slots_ref, out_ref, own_ref):
    copies, cases = out_ref.shape[0], trace_ref.shape[0]
    y = jnp.sum(arrived_ref[...], axis=0)
    own_ref[...] = y
    trace = trace_ref[...]
    r = slots_ref[0]
    d = slots_ref[1]
    dots = dots_ref[...]
    terms = (None, d * y, r * y, (2.0 * trace + y) * y)
    row = jnp.zeros((1, 128), F32)
    for i, term in enumerate(terms):
        column = dots[:, i : i + 1]
        if term is not None:
            column = column + jnp.sum(term, axis=1, keepdims=True)
        row = row + column_to_row(column, i * cases)
    image = trace + y
    rows = jnp.broadcast_to(row, (8, 128))
    for i in range(copies):
        out_ref[i, :cases, :] = image
        out_ref[i, cases:, :] = rows


def range_sum_kernel(cases, mine_ref, other_ref, out_ref):
    row = jnp.sum(mine_ref[:, cases:, :], axis=0) + jnp.sum(other_ref[:, cases:, :], axis=0)
    out_ref[...] = jnp.broadcast_to(row[0:1, :][None], out_ref.shape)


def edges_kernel(own_ref, inverse_ref, *refs):
    edge_refs, new_edge_refs = refs[:4], refs[4:]
    slabs, width = inverse_ref.shape[:2]
    sides = (
        inverse_ref[slabs - 1],
        inverse_ref[0],
        jnp.concatenate([inverse_ref[a, width - 1 :, :] for a in range(slabs)], axis=0),
        jnp.concatenate([inverse_ref[a, :1, :] for a in range(slabs)], axis=0),
    )

    def step(case, carry):
        values = jnp.broadcast_to(own_ref[pl.ds(case, 1), :], (8, 128))
        for slot, edge_ref, new_edge_ref in zip(sides, edge_refs, new_edge_refs):
            there = slot > 0
            extra = lanes_taken(values, jnp.where(there, slot - 1, 0))
            new_edge_ref[case] = edge_ref[case] + jnp.where(there, extra, 0.0)
        return carry

    lax.fori_loop(0, own_ref.shape[0], step, 0, unroll=4)


def last_sums_kernel(arrived_ref, dots_ref, out_ref):
    copies = out_ref.shape[0]
    cases = dots_ref.shape[0]
    total = jnp.sum(arrived_ref[...], axis=0)
    z = total[:cases]
    rest = total[cases:]
    low = z.astype(BF16).astype(F32)
    dots = dots_ref[...]
    curvature = dots[:, 1:2] + jnp.sum((z + rest) * low, axis=1, keepdims=True)
    row = column_to_row(dots[:, 0:1], 0) + column_to_row(curvature, cases)
    out_ref[...] = jnp.broadcast_to(row[None], (copies, 1, 128))


def final_kernel(sums_ref, direction_ref, solution_ref, out_ref, alpha_ref):
    cases, slabs, width = direction_ref.shape[:3]
    row = jnp.sum(sums_ref[...], axis=0)
    norm = row_to_column(row, 0, cases)
    curvature = row_to_column(row, cases, cases)
    alpha_ref[...] = jnp.broadcast_to(norm / curvature, (cases, 128))

    def step(case, carry):
        alpha = jnp.broadcast_to(alpha_ref[pl.ds(case, 1), :], (width, 128))
        for a in range(slabs):
            out_ref[case, a] = solution_ref[case, a] + alpha * direction_ref[case, a]
        return carry

    lax.fori_loop(0, cases, step, 0, unroll=2)


def shards(
    right_side,
    block_weight,
    across_weight,
    along_weight,
    block_stiffness,
    across_matrix,
    along_matrix,
    boundary_blocks,
    block_rows,
    block_columns,
    live_pairs,
    surface_index,
    interface_slot,
):
    cases, slabs, width, lanes = right_side.shape
    field = right_side.shape
    rows_local = block_rows[0, 0]
    columns_local = block_columns[0, 0]
    blocks_local = boundary_blocks[0, 0]
    live_local = live_pairs[0, 0]
    surface_local = surface_index[0, 0]
    half = lax.axis_index("sec").astype(jnp.int32)
    place = lax.axis_index(BLK).astype(jnp.int32)
    blk_count = lax.axis_size(BLK)
    clu_count = lax.axis_size(CLU)
    owners = 2 * blk_count
    all_count = owners * clu_count
    slot_count = interface_slot.shape[0]
    surface = surface_local.reshape(1, lanes)

    def edges_by(make):
        return edge_outputs(cases, slabs, width, lanes, make)

    def sent(edges):
        before = passed_along(edges[0], SEC_CLU, 1)
        after = passed_along(edges[1], SEC_CLU, -1)
        left = passed_along(edges[2], BLK, 1)
        right = passed_along(edges[3], BLK, -1)
        return before, after, left, right

    first_edges = [
        kept((cases + 1, width, lanes)),
        kept((cases, width, lanes)),
        kept((cases + 1, slabs, lanes)),
        kept((cases, slabs, lanes)),
    ]
    trace, *edges = kernel(
        first_trace_kernel,
        (kept((blk_count, cases, lanes)), *first_edges),
        (right_side, surface, across_weight, along_weight),
    )
    mine = exchanged(trace, BLK)
    other = partner(mine)

    owner = (interface_slot // lanes) ^ (half * blk_count)
    slot_blocks = owner.reshape(slot_count // lanes, lanes)
    slot_lanes = (interface_slot % lanes).reshape(slot_count // lanes, lanes)
    number = jnp.arange(slot_count, dtype=jnp.int32)
    lane_number = jnp.arange(lanes, dtype=jnp.int32)
    by_owner = (jnp.arange(owners, dtype=jnp.int32)[:, None] == owner[None, :]).astype(BF16)
    by_lane = (interface_slot % lanes)[:, None] == lane_number[None, :]
    parts = jnp.concatenate(
        [
            jnp.where(by_lane, (number // lanes)[:, None], 0),
            jnp.where(by_lane, (number % lanes)[:, None], 0),
        ],
        axis=1,
    ).astype(BF16)
    found = jnp.dot(by_owner, parts, preferred_element_type=F32).astype(jnp.int32)
    dof_blocks, dof_lanes = found[:, :lanes], found[:, lanes:]
    by_block = (
        jnp.arange(slabs * width, dtype=jnp.int32)[:, None] == (surface_local // lanes)[None, :]
    ).astype(BF16)
    marks = jnp.where(
        (surface_local % lanes)[:, None] == lane_number[None, :],
        jnp.arange(1, surface_local.shape[0] + 1, dtype=jnp.int32)[:, None],
        0,
    ).astype(BF16)
    inverse = (
        jnp.dot(by_block, marks, preferred_element_type=F32)
        .astype(jnp.int32)
        .reshape(slabs, width, lanes)
    )

    matrices = jnp.stack(
        [block_stiffness, across_matrix, across_matrix.T, along_matrix, along_matrix.T]
    )

    half_columns = clu_count
    slots_shape = (owners, cases, lanes)
    pairs = jnp.stack(
        [
            rows_local,
            columns_local ^ (half * half_columns),
            jnp.broadcast_to(live_local, rows_local.shape),
            jnp.broadcast_to(place, rows_local.shape),
        ]
    )
    forward_inputs = (pairs, slot_lanes, slot_blocks, near(blocks_local))

    def weights_of(halo):
        across_edge = halo[0][cases, :, 0][None, :]
        along_edge = halo[2][cases, :, 0][:, None]
        across_lower = jnp.concatenate([across_edge, across_weight[:-1, :]], axis=0)
        along_lower = jnp.concatenate([along_edge, along_weight[:, :-1]], axis=1)
        tile = jnp.arange(width, dtype=jnp.int32)[None, :]
        weights = jnp.stack(
            [
                block_weight,
                across_weight,
                across_lower,
                jnp.where(tile < width - 1, along_weight, 0.0),
                jnp.where(tile > 0, along_lower, 0.0),
                jnp.where(tile == width - 1, along_weight, 0.0),
                jnp.where(tile == 0, along_lower, 0.0),
            ]
        )
        return jnp.broadcast_to(weights[..., None], (*weights.shape, lanes))

    edge_kept, edge_like = edges_by(kept), edges_by(like)
    own_slots_shape = steps_shape = like((2, cases, lanes))
    image_outputs = (like(field), like((cases, lanes)), like((cases, lanes)), *edge_like)
    stiffness_scratch = [pltpu.VMEM((cases, slabs, lanes), F32)] * 2
    stiffness_scratch += [pltpu.VMEM((4, cases, lanes), F32)]
    solution = None
    residual = right_side
    direction = right_side
    slot_residual = slot_direction = sums = None
    for iteration in range(ITERS):
        first = iteration == 0
        last = iteration + 1 == ITERS
        deep = 2 * cases if last else cases
        scratch = [
            pltpu.VMEM((slot_count // lanes, deep, lanes), BF16),
            pltpu.VMEM((2 * half_columns, deep, lanes), F32),
            pltpu.VMEM((owners * cases, 2 * lanes if last else lanes), BF16),
        ]
        halves = (kept((half_columns, deep, lanes)),) * 2
        if not first:
            inputs = (*forward_inputs, slot_residual, slot_direction)
            inputs += (near(mine), near(other), near(sums))
            if last:
                steps, keep, send = kernel(
                    functools.partial(forward_kernel, False, True),
                    (steps_shape, *halves),
                    inputs,
                    [pltpu.VMEM(slots_shape, F32)] + scratch,
                    1,
                )
            else:
                steps, slot_residual, slot_direction, own_slots, keep, send = kernel(
                    functools.partial(forward_kernel, False, False),
                    (steps_shape, *(like(slots_shape),) * 2, own_slots_shape, *halves),
                    inputs,
                    scratch,
                    1,
                )
        if first:
            slot_direction, own_slots, keep, send = kernel(
                functools.partial(forward_kernel, True, False),
                (like(slots_shape), own_slots_shape, *halves),
                (*forward_inputs, near(mine), near(other)),
                scratch,
                1,
            )
            slot_residual = slot_direction
        pieces = keep + partner(send)
        column_pieces = exchanged(pieces, CLU)

        if first:
            halo_residual = halo_direction = sent(edges)
            given = (weights_of(halo_direction), matrices, surface)
            image, dots, image_trace, *edges = kernel(
                functools.partial(stiffness_kernel, True),
                image_outputs,
                (right_side, *halo_direction, *given),
                stiffness_scratch,
            )
        else:
            inputs = (steps, own, inverse, image, residual, direction)
            if iteration > 1:
                inputs += (solution,)
            inputs += (*halo_image, *halo_residual, *halo_direction)
            if last:
                solution, direction, dots = kernel(
                    functools.partial(field_kernel, iteration == 1, True),
                    (like(field), like(field), like((cases, lanes))),
                    (*inputs, *given),
                    [pltpu.VMEM(field, F32)] * 2
                    + [pltpu.VMEM(edge.shape, F32) for edge in halo_image]
                    + stiffness_scratch,
                )
            else:
                outs = kernel(
                    functools.partial(field_kernel, iteration == 1, False),
                    (like(field),) * 3 + edge_like * 2,
                    inputs,
                )
                solution, direction, residual = outs[:3]
                halo_residual, halo_direction = outs[3:7], outs[7:11]
            if not last:
                image, dots, image_trace, *edges = kernel(
                    functools.partial(stiffness_kernel, False),
                    image_outputs,
                    (direction, residual, *halo_direction, *given),
                    stiffness_scratch,
                )
        if last:
            rows = kernel(
                last_sums_kernel, kept((all_count, 1, lanes)), (near(column_pieces), dots)
            )
            totals = exchanged(rows, ALL)
            return kernel(
                final_kernel,
                like(field),
                (near(totals), direction, solution),
                [pltpu.VMEM((cases, lanes), F32)],
            )

        z_low = kernel(low_kernel, kept((clu_count, cases, lanes), BF16), (near(column_pieces),))
        low_mine = exchanged(z_low, CLU)
        low_other = partner(low_mine)
        keep, send = kernel(
            backward_kernel,
            (kept((blk_count, cases, lanes)),) * 2,
            (
                pairs,
                dof_lanes,
                dof_blocks,
                near(blocks_local),
                near(low_mine),
                near(low_other),
            ),
            [
                pltpu.VMEM((2 * half_columns, cases, lanes), BF16),
                pltpu.VMEM((slot_count // lanes, cases, lanes), F32),
            ],
            1,
        )
        row_pieces = keep + partner(send)
        arrived = exchanged(row_pieces, BLK)
        payload, own = kernel(
            own_kernel,
            (kept((blk_count, cases + 8, lanes)), like((cases, lanes))),
            (near(arrived), image_trace, dots, own_slots),
        )
        mine = exchanged(payload, BLK)
        edges = kernel(edges_kernel, edge_kept, (own, inverse, *edges))
        halo_image = sent(edges)
        other = partner(mine)
        row = kernel(
            functools.partial(range_sum_kernel, cases),
            kept((clu_count, 1, lanes)),
            (near(mine), near(other)),
        )
        sums = exchanged(row, CLU)


def solution(mesh):
    finer = Mesh(
        mesh.devices.reshape(mesh.shape["sec"], 4, 2, 2, 8),
        ("sec", "clu_0", "clu_1", "blk_0", "blk_1"),
    )
    placed = (
        P(None, SEC_CLU, BLK, None),
        P(SEC_CLU, BLK),
        P(SEC_CLU, BLK),
        P(SEC_CLU, BLK),
        P(),
        P(),
        P(),
        P("sec", CLU, BLK, None, None),
        P("sec", CLU, BLK),
        P("sec", CLU, BLK),
        P("sec", CLU, BLK),
        P("sec", CLU, BLK),
        P(CLU),
    )
    return jax.shard_map(
        shards, mesh=finer, in_specs=placed, out_specs=P(None, SEC_CLU, BLK, None), check_vma=False
    )
```
